32 devices in a mesh: grp: 2 (over x), tm: 16 (over z, y, core).
Axes of the slice: x: 2, y: 2, z: 4, core: 2. Of those that a mesh axis runs over, the one named last changes fastest.
Arguments:
- queries: bfloat16 [2, 8192, 1120], P(None, ('grp', 'tm')), parts along dimension 1, may hold values from 0.19921875 to 3
- keys: bfloat16 [2, 8192, 1120], P(None, ('grp', 'tm')), parts along dimension 1, may hold values from 0.05 to 24
- values: bfloat16 [2, 8192, 1120], P(None, ('grp', 'tm')), parts along dimension 1, may hold values from -12 to 12
- timesteps: int32 [4], P('grp'), parts along dimension 0, may hold values from 0 to 19
- gate_table: float32 [20, 2240], replicated, may hold values from -3 to 3
- out_weight: bfloat16 [1120, 2240], replicated, may hold values from -0.1875 to 0.1875
- conv_weight: float32 [9, 1120], replicated, may hold values from -1.5 to 1.5
Outputs:
- update: float32 [2, 8192, 2240], P(None, ('grp', 'tm')), parts along dimension 1
- fresh_state: float32 [32, 70, 70], P('grp'), parts along dimension 0
- fresh_total: float32 [32, 70], P('grp'), parts along dimension 0
The draws below stay inside these ranges and needn't reach their ends.
There are 2 independent parts, one for each index of `grp`. The reference program is written for one: setup_inputs(seed, part) draws one part's arguments, and reference() takes and returns one part's arrays. A program takes and returns all parts, laid end to end along the dimension named above; an argument that names none is the same for every part. Nothing has to cross between parts.
All inputs are finite; a program needn't handle non-finite values.
Results may differ from the reference program's by a relative error of at most 0.0003.
The reference program's roundings to bfloat16 on the way count: a program that leaves them out, or rounds other values in their place, can miss the bound.
Values may be sent and summed in bfloat16 or wider, within the bound.
No kernel may reach another device: no remote copies, remote signals or barrier semaphores. Data moves between devices by JAX's collectives and lax.ppermute only.
A program may use at most 64 MiB of HBM per device.

```python
import math
import jax
import jax.numpy as jnp
from jax import lax

D = 2240
NH = 16
HD = 70
COLS = 64
NSTEPS = 20
ROWS_DEV = 4
FRAME_ROWS = 64
TOKENS = 4096
N_TM = 16


def both_fields(key):
    subkeys = jax.random.split(jax.random.fold_in(key, 11), 7)
    channels = NH * HD
    row_total = TOKENS // COLS
    row_ids = (jnp.arange(TOKENS, dtype=jnp.int32) // COLS).astype(jnp.float32)
    rise = (1.0 + 2.0 * row_ids / (row_total - 1.0))[:, None]
    log_keys = jax.random.uniform(subkeys[0], (TOKENS, channels), jnp.float32, -1.0, 1.0) + 0.5 * jax.random.normal(subkeys[1], (1, channels), jnp.float32)
    jitter = jax.random.normal(subkeys[2], (TOKENS, channels), jnp.float32)
    common = jax.random.normal(subkeys[3], (1, channels), jnp.float32)
    offsets = 0.7 * jax.random.normal(subkeys[4], (row_total, channels), jnp.float32)
    key_first = jnp.exp(log_keys) * rise
    key_second = key_first * jnp.exp(0.3 * jax.random.normal(subkeys[5], (TOKENS, channels), jnp.float32))
    value_first = jitter + common + jnp.repeat(offsets, COLS, axis=0)
    value_second = value_first + 0.5 * jax.random.normal(subkeys[6], (TOKENS, channels), jnp.float32)
    key_pair = jnp.clip(jnp.stack([key_first, key_second]), 0.05, 24.0)
    value_pair = jnp.clip(jnp.stack([value_first, value_second]), -12.0, 12.0)
    return (key_pair, value_pair)


def draw_keys(key, part):
    return both_fields(key)[0].astype(jnp.bfloat16)


def draw_values(key, part):
    return both_fields(key)[1].astype(jnp.bfloat16)


def shard_levels(rng, shape, cuts, smallest, high):
    def one(dim, shards_of):
        draws = jax.random.uniform(jax.random.fold_in(jax.random.fold_in(rng, 6), dim), (shards_of,), jnp.float32, smallest / len(cuts), high / len(cuts))
        return jnp.repeat(jnp.exp(draws), shape[dim] // shards_of).reshape((-1,) + (1,) * (len(shape) - dim - 1))

    gain = one(*cuts[0])
    for cut in cuts[1:]:
        gain = gain * one(*cut)
    return gain


def scatter_about(stream_key, shape, width, bound, held_as=jnp.bfloat16):
    return jnp.clip(width * jax.random.normal(stream_key, shape, jnp.float32), -bound, bound).astype(held_as)


def setup_inputs(seed: int = 0, part: int = 0) -> dict:
    streams_of = jax.random.split(jax.random.key(seed), 8)
    part_splits = jax.random.split(jax.random.fold_in(streams_of[7], part), 8)
    return {
        "queries": jnp.clip(jnp.exp(math.log(3.0) - 2.7119641 * jax.random.uniform(part_splits[0], (2, TOKENS, NH * HD), jnp.float32) ** shard_levels(part_splits[0], (2, TOKENS, NH * HD), ((1, 16),), -0.2, 0.2)), 0.19921875, 3.0).astype(jnp.bfloat16),
        "keys": draw_keys(jax.random.fold_in(jax.random.fold_in(streams_of[7], part), 71), part),
        "values": draw_values(jax.random.fold_in(jax.random.fold_in(streams_of[7], part), 71), part),
        "timesteps": jax.random.randint(part_splits[3], (2,), 0, NSTEPS).astype(jnp.int32),
        "gate_table": scatter_about(streams_of[4], (NSTEPS, D), 0.6, 3.0, jnp.float32),
        "out_weight": scatter_about(streams_of[5], (NH * HD, D), (NH * HD) ** -0.5, 0.1875),
        "conv_weight": scatter_about(streams_of[6], (9, NH * HD), 0.3, 1.5, jnp.float32),
    }


EXACT = lax.Precision.HIGHEST


def select_gate(gate_table, position):
    step_ids = jnp.arange(gate_table.shape[0], dtype=jnp.int32)
    return jnp.sum(jnp.where((step_ids == position)[:, None], gate_table, jnp.zeros_like(gate_table)), axis=0)


def shard_states(key_rows, values):
    key_grid = key_rows.astype(jnp.float32).reshape(N_TM, -1, NH, HD)
    value_grid = values.astype(jnp.float32).reshape(N_TM, -1, NH, HD)
    key_state = jnp.einsum('jrhd,jrhe->jhde', key_grid, value_grid, precision=EXACT)
    key_total = jnp.sum(key_grid, axis=1)
    return key_state, key_total


def spread(queries, key_state, key_total):
    query_grid = queries.astype(jnp.float32).reshape(N_TM, -1, NH, HD)
    numer = jnp.einsum('jrhd,jhde->jrhe', query_grid, key_state, precision=EXACT)
    denom = jnp.einsum('jrhd,jhd->jrh', query_grid, key_total, precision=EXACT)
    return (numer / denom[..., None]).reshape(-1, NH * HD)


def rim_rows(rims):
    per_frame = FRAME_ROWS // ROWS_DEV
    shard_ids = jnp.arange(N_TM, dtype=jnp.int32)
    upper_rim = jnp.concatenate([jnp.zeros_like(rims[:1, -1]), rims[:-1, -1]], axis=0)
    lower_rim = jnp.concatenate([rims[1:, 0], jnp.zeros_like(rims[:1, 0])], axis=0)
    upper_rim = jnp.where((shard_ids % per_frame != 0)[:, None, None], upper_rim, jnp.zeros_like(upper_rim))
    lower_rim = jnp.where(((shard_ids + 1) % per_frame != 0)[:, None, None], lower_rim, jnp.zeros_like(lower_rim))
    return upper_rim, lower_rim


def convolve(center, upper_rim, lower_rim, conv_weight):
    padded = jnp.concatenate([upper_rim[:, None], center, lower_rim[:, None]], axis=1).astype(jnp.float32)
    padded = jnp.pad(padded, ((0, 0), (0, 0), (1, 1), (0, 0)))
    summed = jnp.zeros(center.shape, jnp.float32)
    for tap_row in range(3):
        for tap_col in range(3):
            summed = summed + padded[:, tap_row:tap_row + ROWS_DEV, tap_col:tap_col + COLS] * conv_weight[3 * tap_row + tap_col]
    return summed.reshape(-1, center.shape[-1])


def reference(queries, keys, values, timesteps, gate_table, out_weight, conv_weight):
    channels = NH * HD
    gates = [select_gate(gate_table, timesteps[section]) for section in range(2)]
    state_one, total_one = shard_states(keys[0], values[0])
    state_two, total_two = shard_states(keys[1], values[1])
    whole_state = jnp.sum(state_one, axis=0)
    whole_total = jnp.sum(total_one, axis=0)
    fresh_state = jnp.sum(state_two, axis=0) / TOKENS
    fresh_total = jnp.sum(total_two, axis=0) / TOKENS
    shared_state = jnp.broadcast_to(whole_state, state_one.shape)
    shared_total = jnp.broadcast_to(whole_total, total_one.shape)
    moved_state = whole_state[None] - state_one + state_two
    moved_total = whole_total[None] - total_one + total_two
    grid_one = values[0].reshape(N_TM, ROWS_DEV, COLS, channels)
    grid_two = values[1].reshape(N_TM, ROWS_DEV, COLS, channels)
    upper_rim, lower_rim = rim_rows(grid_one)
    mixed_one = (spread(queries[0], shared_state, shared_total) + convolve(grid_one, upper_rim, lower_rim, conv_weight)).astype(jnp.bfloat16)
    mixed_two = (spread(queries[1], moved_state, moved_total) + convolve(grid_two, upper_rim, lower_rim, conv_weight)).astype(jnp.bfloat16)
    update_one = gates[0] * jnp.dot(mixed_one, out_weight, preferred_element_type=jnp.float32)
    update_two = gates[1] * jnp.dot(mixed_two, out_weight, preferred_element_type=jnp.float32)
    return jnp.stack([update_one, update_two]), fresh_state, fresh_total
```

```python
import functools

import jax
import jax.numpy as jnp
from jax import lax
from jax.experimental import pallas as pl
from jax.experimental.pallas import tpu as pltpu
from jax.sharding import PartitionSpec as P

NH = 16
HD = 70
COLS = 64
ROWS_DEV = 4

F32 = jnp.float32
BF16 = jnp.bfloat16
LANES = 128
HALF_HEADS = NH // 2
HALF = HALF_HEADS * HD
TOK = ROWS_DEV * COLS
FULL_TILES = HALF // LANES
TILE_BASE = [LANES * j for j in range(FULL_TILES)] + [HALF - LANES]
REST = HALF - LANES * FULL_TILES
TROWS = 72
FOLD = 40
PACKED = FULL_TILES * TROWS + FOLD
LIMIT = 48 << 20


def tiles_of(head):
    first, last = HD * head, HD * head + HD
    return [j for j in range(FULL_TILES + 1) if first < min(LANES * j + LANES, HALF) and last > LANES * j]


def lane_mask(shape, tile, head):
    chan = TILE_BASE[tile] + lax.broadcasted_iota(jnp.int32, shape, 1)
    low = max(HD * head, LANES * tile)
    return (chan >= low) & (chan < HD * head + HD)


def nt_dot(a, b):
    return lax.dot_general(a, b, (((1,), (1,)), ((), ())), preferred_element_type=F32)


def pack_states(keys, values, out_ref):
    acc = [jnp.zeros((TROWS, LANES), F32) for _ in TILE_BASE]
    rows = lax.broadcasted_iota(jnp.int32, (TROWS, LANES), 0)
    for head in range(HALF_HEADS):
        start = HD * head // 16 * 16
        stop = min(HALF, -(-(HD * head + HD) // 16) * 16)
        shift = HD * head - start
        for tile in tiles_of(head):
            base = TILE_BASE[tile]
            prod = nt_dot(values[start:stop], keys[base : base + LANES])
            part = jnp.concatenate([prod[shift : shift + HD], jnp.zeros((TROWS - HD, LANES), F32)], axis=0)
            acc[tile] = jnp.where(lane_mask((TROWS, LANES), tile, head), part, acc[tile])
    ones = jnp.ones((16, TOK), BF16)
    for tile, base in enumerate(TILE_BASE):
        total = nt_dot(ones, keys[base : base + LANES])[:1]
        acc[tile] = jnp.where(rows == HD, jnp.broadcast_to(total, (TROWS, LANES)), acc[tile])
    for tile in range(FULL_TILES):
        out_ref[tile * TROWS : (tile + 1) * TROWS] = acc[tile]
    last = acc[FULL_TILES]
    low = jnp.concatenate([last[FOLD:], jnp.zeros((2 * FOLD - TROWS, LANES), F32)], axis=0)
    lanes = lax.broadcasted_iota(jnp.int32, (FOLD, LANES), 1)
    out_ref[FULL_TILES * TROWS :] = jnp.where(lanes >= LANES - REST, last[:FOLD], pltpu.roll(low, LANES // 2, 1))


def unpack_tiles(packed):
    tiles = [packed[j * TROWS : (j + 1) * TROWS] for j in range(FULL_TILES)]
    fold = packed[FULL_TILES * TROWS :]
    tiles.append(jnp.concatenate([fold, pltpu.roll(fold, LANES // 2, 1)[: TROWS - FOLD]], axis=0))
    return tiles


def split3(x):
    one = x.astype(BF16)
    rest = x - one.astype(F32)
    two = rest.astype(BF16)
    three = (rest - two.astype(F32)).astype(BF16)
    return one, two, three


def state_kernel(core, key_ref, value_ref, out_ref):
    pack_states(key_ref[0], value_ref[0], out_ref.at[0])


def local_states(core, keys, values, picks):
    def pick(i, core):
        step, own = 0, 0
        for n, (s, o) in enumerate(picks):
            step = jnp.where(i == n, s, step)
            own = jnp.where(i == n, o, own)
        half = jnp.where(own == 1, core[0], 1 - core[0])
        return step, half, 0

    spec = pl.BlockSpec((1, HALF, TOK), pick)
    return pl.pallas_call(
        state_kernel,
        out_shape=jax.ShapeDtypeStruct((len(picks), PACKED, LANES), F32),
        grid_spec=pltpu.PrefetchScalarGridSpec(
            num_scalar_prefetch=1,
            grid=(len(picks),),
            in_specs=[spec, spec],
            out_specs=pl.BlockSpec((1, PACKED, LANES), lambda i, core: (i, 0, 0)),
        ),
        compiler_params=pltpu.CompilerParams(vmem_limit_bytes=LIMIT),
        cost_estimate=pl.CostEstimate(flops=10_000_000, bytes_accessed=600_000 * len(picks), transcendentals=0),
        name="local_states",
    )(core, keys, values)


def rim_kernel(core_ref, value_ref, near_ref, far_ref):
    lanes = lax.broadcasted_iota(jnp.int32, (HALF, LANES), 1)
    left = lanes < COLS
    first = core_ref[0] == 0
    top = value_ref[0, :HALF, :LANES].astype(F32)
    bottom = value_ref[0, HALF:, :LANES].astype(F32)
    head = jnp.where(left, top, pltpu.roll(bottom, COLS, 1))
    top = value_ref[0, :HALF, TOK - LANES :].astype(F32)
    bottom = value_ref[0, HALF:, TOK - LANES :].astype(F32)
    tail = jnp.where(left, pltpu.roll(top, COLS, 1), bottom)
    near_ref[...] = jnp.where(first, tail, head).astype(BF16)
    far_ref[...] = jnp.where(first, head, tail).astype(BF16)


def rims(core, values):
    shape = jax.ShapeDtypeStruct((HALF, LANES), BF16)
    return pl.pallas_call(
        rim_kernel,
        out_shape=(shape, shape),
        grid_spec=pltpu.PrefetchScalarGridSpec(
            num_scalar_prefetch=1,
            grid=(1,),
            in_specs=[pl.BlockSpec((1, 2 * HALF, TOK), lambda i, core: (0, 0, 0))],
            out_specs=[pl.BlockSpec((HALF, LANES), lambda i, core: (0, 0))] * 2,
        ),
        name="rims",
    )(core, values)


GROUP = 16


def conv_kernel(core_ref, value_ref, near_ref, far_ref, weight_ref, out_ref, taps):
    half = pl.program_id(0)
    taps[...] = weight_ref[...].T
    lanes = lax.broadcasted_iota(jnp.int32, (GROUP, LANES), 1)
    left = lanes < COLS
    inner_left = (lanes != 0) & (lanes != COLS)
    inner_right = (lanes != COLS - 1) & (lanes != LANES - 1)
    first = core_ref[0] == 0
    low_half = half == 0

    def turn(x):
        return pltpu.roll(x, COLS, 1)

    def group(i, carry):
        row = pl.multiple_of(i * GROUP, GROUP)
        near = near_ref[pl.ds(row, GROUP)].astype(F32)
        far = far_ref[pl.ds(row, GROUP)].astype(F32)
        above = jnp.where(first, far, near)
        below = jnp.where(first, near, far)
        rim = jnp.where(
            left, jnp.where(low_half, above, turn(above)), jnp.where(low_half, turn(below), below)
        )
        tap = taps[pl.ds(row, GROUP)]
        weights = []
        for k in range(9):
            w = jnp.broadcast_to(tap[:, k : k + 1], (GROUP, LANES))
            if k % 3 == 0:
                w = jnp.where(inner_left, w, 0.0)
            if k % 3 == 2:
                w = jnp.where(inner_right, w, 0.0)
            weights.append(w)
        for step in range(2):
            a = value_ref[step, pl.ds(row, GROUP), :LANES].astype(F32)
            b = value_ref[step, pl.ds(row, GROUP), LANES:].astype(F32)
            ta, tb = turn(a), turn(b)
            lines = [
                jnp.where(left, rim, ta),
                a,
                jnp.where(left, ta, tb),
                b,
                jnp.where(left, tb, rim),
            ]
            wide = [(pltpu.roll(x, 1, 1), x, pltpu.roll(x, LANES - 1, 1)) for x in lines]
            for part in range(2):
                total = None
                for r in range(3):
                    for c in range(3):
                        term = wide[2 * part + r][c] * weights[3 * r + c]
                        total = term if total is None else total + term
                out_ref[step, pl.ds(row, GROUP), part * LANES : (part + 1) * LANES] = total
        return carry

    lax.fori_loop(0, HALF // GROUP, group, 0)


def convolve(core, values, near, far, weights):
    return pl.pallas_call(
        conv_kernel,
        out_shape=jax.ShapeDtypeStruct((2, 2 * HALF, TOK), F32),
        grid_spec=pltpu.PrefetchScalarGridSpec(
            num_scalar_prefetch=1,
            grid=(2,),
            in_specs=[
                pl.BlockSpec((2, HALF, TOK), lambda i, core: (0, i, 0)),
                pl.BlockSpec((HALF, LANES), lambda i, core: (0, 0)),
                pl.BlockSpec((HALF, LANES), lambda i, core: (0, 0)),
                pl.BlockSpec((None, 9, HALF), lambda i, core: (i, 0, 0)),
            ],
            out_specs=pl.BlockSpec((2, HALF, TOK), lambda i, core: (0, i, 0)),
            scratch_shapes=[pltpu.VMEM((HALF, 9), F32)],
        ),
        compiler_params=pltpu.CompilerParams(vmem_limit_bytes=LIMIT),
        cost_estimate=pl.CostEstimate(flops=12_000_000, bytes_accessed=3_500_000, transcendentals=0),
        name="convolve",
    )(core, values, near, far, weights)


def mix_kernel(chunks, core_ref, step_ref, query_hbm, conv_hbm, weight_hbm, gate_ref,
               own_ref, other_ref, keep0, send0, keep1, send1, out_hbm,
               query, acc, weight, mixed, result, sem_in, sem_out):
    loads = [
        pltpu.make_async_copy(query_hbm, query, sem_in.at[0]),
        pltpu.make_async_copy(conv_hbm, acc, sem_in.at[1]),
        pltpu.make_async_copy(weight_hbm, weight, sem_in.at[2]),
    ]
    for load in loads:
        load.start()
    gate_rows = [gate_ref[pl.ds(step_ref[s], 1), :] for s in range(2)]
    gates = jnp.concatenate(gate_rows + [gate_rows[0]] * 6, axis=0).T
    waited = False
    for part, (whole_ref, zero_ref, one_ref) in enumerate(((own_ref, keep0, keep1), (other_ref, send0, send1))):
        half = core_ref[0] if part == 0 else 1 - core_ref[0]
        base = half * HALF
        whole = whole_ref[...]
        states = (whole, whole - zero_ref[0] + one_ref[0])
        for step in range(2):
            tiles = unpack_tiles(states[step])
            if not waited:
                loads[0].wait()
                loads[1].wait()
                waited = True
            rows8 = lax.broadcasted_iota(jnp.int32, (HALF_HEADS, LANES), 0)
            den = None
            for tile, packed in enumerate(tiles):
                owner = jnp.zeros((HALF_HEADS, LANES), jnp.bool_)
                for head in range(HALF_HEADS):
                    if tile in tiles_of(head):
                        owner = owner | (lane_mask((HALF_HEADS, LANES), tile, head) & (rows8 == head))
                row = jnp.where(owner, jnp.broadcast_to(packed[HD : HD + 1], (HALF_HEADS, LANES)), 0.0)
                q = query[step, pl.ds(pl.multiple_of(base + TILE_BASE[tile], 16), LANES)]
                left = jnp.concatenate([x.astype(F32) for x in split3(row)] + [jnp.zeros((HALF_HEADS, LANES), F32)], axis=0).astype(BF16)
                got = jnp.dot(left, q, preferred_element_type=F32)
                got = got[:8] + got[8:16] + got[16:24]
                den = got if den is None else den + got
            inverse = 1.0 / den
            for head in range(HALF_HEADS):
                first = HD * head // 8 * 8
                shift = HD * head - first
                count = -(-(shift + HD) // 8) * 8
                rows = lax.broadcasted_iota(jnp.int32, (TROWS, LANES), 0)
                total = None
                for tile in tiles_of(head):
                    block = jnp.where(lane_mask((TROWS, LANES), tile, head) & (rows < HD), tiles[tile], 0.0)
                    block = jnp.concatenate([block, jnp.zeros((80 - TROWS, LANES), F32)], axis=0)
                    if shift:
                        block = jnp.concatenate([block[80 - shift :], block[: 80 - shift]], axis=0)
                    left = jnp.concatenate(split3(block), axis=0)
                    q = query[step, pl.ds(pl.multiple_of(base + TILE_BASE[tile], 16), LANES)]
                    got = jnp.dot(left, q, preferred_element_type=F32)
                    got = got[:80] + got[80:160] + got[160:]
                    total = got if total is None else total + got
                spot = pl.ds(pl.multiple_of(base + first, 8), count)
                acc[step, spot] = acc[step, spot] + total[:count] * inverse[head : head + 1]
    for step in range(2):
        mixed[:, step * TOK : (step + 1) * TOK] = acc[step].astype(BF16)
    loads[2].wait()
    stores = []
    for n, (start, size) in enumerate(chunks):
        prod = lax.dot_general(
            weight[:, start : start + size], mixed[...], (((0,), (0,)), ((), ())), preferred_element_type=F32
        )
        for step in range(2):
            result[step, start : start + size] = (
                prod[:, step * TOK : (step + 1) * TOK] * gates[start : start + size, step : step + 1]
            )
            stores.append(
                pltpu.make_async_copy(
                    result.at[step, start : start + size], out_hbm.at[step, start : start + size], sem_out.at[n, step]
                )
            )
            stores[-1].start()
    for store in stores:
        store.wait()


def mix(core, timesteps, queries, conv, weight, gate_table, own, other, keep0, send0, keep1, send1):
    width = weight.shape[1]
    chunks = [(s, min(256, width - s)) for s in range(0, width, 256)]
    smem = pl.BlockSpec(memory_space=pltpu.SMEM)
    anyspace = pl.BlockSpec(memory_space=pl.ANY)
    vmem = pl.BlockSpec(memory_space=pltpu.VMEM)
    return pl.pallas_call(
        functools.partial(mix_kernel, chunks),
        out_shape=jax.ShapeDtypeStruct((2, width, TOK), F32),
        in_specs=[smem, smem, anyspace, anyspace, anyspace] + [vmem] * 7,
        out_specs=anyspace,
        scratch_shapes=[
            pltpu.VMEM((2, 2 * HALF, TOK), BF16),
            pltpu.VMEM((2, 2 * HALF, TOK), F32),
            pltpu.VMEM((2 * HALF, width), BF16),
            pltpu.VMEM((2 * HALF, 2 * TOK), BF16),
            pltpu.VMEM((2, width, TOK), F32),
            pltpu.SemaphoreType.DMA((3,)),
            pltpu.SemaphoreType.DMA((len(chunks), 2)),
        ],
        compiler_params=pltpu.CompilerParams(vmem_limit_bytes=LIMIT),
        cost_estimate=pl.CostEstimate(flops=3_000_000_000, bytes_accessed=14_000_000, transcendentals=0),
        name="mix",
    )(core, timesteps, queries, conv, weight, gate_table, own, other, keep0, send0, keep1, send1)


def fresh_kernel(scale, core_ref, own_ref, other_ref, state_ref, total_ref):
    first = core_ref[0] == 0
    own, other = own_ref[...], other_ref[...]
    halves = (jnp.where(first, own, other), jnp.where(first, other, own))
    lanes = lax.broadcasted_iota(jnp.int32, (TROWS, LANES), 1)
    for half, packed in enumerate(halves):
        tiles = unpack_tiles(packed * scale)
        for head in range(HALF_HEADS):
            block = None
            for tile in tiles_of(head):
                low = max(HD * head, LANES * tile)
                turn = (HD * head - TILE_BASE[tile]) % LANES
                moved = pltpu.roll(tiles[tile], (LANES - turn) % LANES, 1) if turn else tiles[tile]
                block = moved if block is None else jnp.where(lanes >= low - HD * head, moved, block)
            at = half * HALF_HEADS + head
            total_ref[at : at + 1, :] = block[HD : HD + 1, :HD]
            state_ref[:, at, :] = block.T[:HD, :HD]


def fresh(core, own, other, tokens):
    return pl.pallas_call(
        functools.partial(fresh_kernel, 1.0 / tokens),
        out_shape=(jax.ShapeDtypeStruct((HD, NH, HD), F32), jax.ShapeDtypeStruct((NH, HD), F32)),
        in_specs=[pl.BlockSpec(memory_space=pltpu.SMEM)] + [pl.BlockSpec(memory_space=pltpu.VMEM)] * 2,
        out_specs=(pl.BlockSpec(memory_space=pltpu.VMEM),) * 2,
        compiler_params=pltpu.CompilerParams(vmem_limit_bytes=LIMIT),
        name="fresh",
    )(core, own, other)


def local(queries, keys, values, timesteps, gate_table, out_weight, conv_weight):
    count = lax.axis_size("tm")
    tokens = queries.shape[1] * count
    core = (lax.axis_index("tm") % 2).astype(jnp.int32).reshape(1)
    queries, keys, values = (x.transpose(0, 2, 1) for x in (queries, keys, values))

    def swap(x, pick):
        return lax.ppermute(x, "tm", [(i, i ^ pick(i % 2)) for i in range(count)])

    def partner(x):
        return swap(x, lambda c: 1)

    bits = [1 << b for b in range(1, count.bit_length() - 1)]
    turned = bits[-1:] + bits[:-1]
    rounds = [lambda c, b=b, t=t: t if c else b for b, t in zip(bits, turned)]

    send0 = local_states(core, keys, values, ((0, 0),))
    got0 = partner(send0)
    near, far = rims(core, values)
    near = partner(near)
    rest = local_states(core, keys, values, ((0, 1), (1, 0), (1, 1)))
    keep0, send1, keep1 = rest[0:1], rest[1:2], rest[2:3]
    links = [p for i in range(1, count - 1, 2) for p in ((i, i + 1), (i + 1, i))]
    far = lax.ppermute(far, "tm", links)
    conv = convolve(core, values, near, far, conv_weight.reshape(9, 2, HALF).transpose(1, 0, 2))
    whole = keep0[0] + got0[0]
    second = keep1[0] + partner(send1)[0]
    for pick in rounds:
        whole = whole + swap(whole, pick)
        second = second + swap(second, pick)
    other = partner(whole)
    update = mix(core, timesteps, queries, conv, out_weight, gate_table, whole, other, keep0, send0, keep1, send1)
    fresh_state, fresh_total = fresh(core, second, partner(second), tokens)
    return update.transpose(0, 2, 1), fresh_state.transpose(1, 0, 2), fresh_total


def solution(mesh):
    placed = (
        P(None, ("grp", "tm"), None),
        P(None, ("grp", "tm"), None),
        P(None, ("grp", "tm"), None),
        P("grp"),
        P(),
        P(),
        P(),
    )
    return jax.shard_map(
        local,
        mesh=mesh,
        in_specs=placed,
        out_specs=(P(None, ("grp", "tm"), None), P("grp", None, None), P("grp", None)),
        check_vma=False,
    )
```

```python
import functools

import jax
import jax.numpy as jnp
from jax import lax
from jax.experimental.layout import Layout, with_layout_constraint
from jax.experimental import pallas as pl
from jax.experimental.pallas import tpu as pltpu
from jax.sharding import PartitionSpec as P


NH = 16
HD = 70
COLS = 64
ROWS_DEV = 4

F32 = jnp.float32
BF16 = jnp.bfloat16
LANES = 128
HALF_HEADS = NH // 2
HALF = HALF_HEADS * HD
TOK = ROWS_DEV * COLS
FULL_TILES = HALF // LANES
TILE_BASE = [LANES * j for j in range(FULL_TILES)] + [HALF - LANES]
REST = HALF - LANES * FULL_TILES
TROWS = 72
FOLD = 40
SLAB = 80
PACKED = FULL_TILES * TROWS + FOLD
LIMIT = 48 << 20


def tiles_of(head):
    first, last = HD * head, HD * head + HD
    return [j for j in range(FULL_TILES + 1) if first < min(LANES * j + LANES, HALF) and last > LANES * j]


def lane_mask(shape, tile, head):
    chan = TILE_BASE[tile] + lax.broadcasted_iota(jnp.int32, shape, 1)
    low = max(HD * head, LANES * tile)
    return (chan >= low) & (chan < HD * head + HD)


def nt_dot(a, b):
    return lax.dot_general(a, b, (((1,), (1,)), ((), ())), preferred_element_type=F32)


def pack_states(keys, values, out_ref):
    acc = [jnp.zeros((TROWS, LANES), F32) for _ in TILE_BASE]
    rows = lax.broadcasted_iota(jnp.int32, (TROWS, LANES), 0)
    for head in range(HALF_HEADS):
        start = HD * head // 16 * 16
        stop = min(HALF, -(-(HD * head + HD) // 16) * 16)
        shift = HD * head - start
        for tile in tiles_of(head):
            base = TILE_BASE[tile]
            prod = nt_dot(values[start:stop], keys[base : base + LANES])
            part = jnp.concatenate([prod[shift : shift + HD], jnp.zeros((TROWS - HD, LANES), F32)], axis=0)
            acc[tile] = jnp.where(lane_mask((TROWS, LANES), tile, head), part, acc[tile])
    ones = jnp.ones((16, TOK), BF16)
    for tile, base in enumerate(TILE_BASE):
        total = nt_dot(ones, keys[base : base + LANES])[:1]
        acc[tile] = jnp.where(rows == HD, jnp.broadcast_to(total, (TROWS, LANES)), acc[tile])
    for tile in range(FULL_TILES):
        out_ref[tile * TROWS : (tile + 1) * TROWS] = acc[tile]
    last = acc[FULL_TILES]
    low = jnp.concatenate([last[FOLD:], jnp.zeros((2 * FOLD - TROWS, LANES), F32)], axis=0)
    lanes = lax.broadcasted_iota(jnp.int32, (FOLD, LANES), 1)
    out_ref[FULL_TILES * TROWS :] = jnp.where(lanes >= LANES - REST, last[:FOLD], pltpu.roll(low, LANES // 2, 1))


def unpack_tiles(packed):
    tiles = [packed[j * TROWS : (j + 1) * TROWS] for j in range(FULL_TILES)]
    fold = packed[FULL_TILES * TROWS :]
    tiles.append(jnp.concatenate([fold, pltpu.roll(fold, LANES // 2, 1)[: TROWS - FOLD]], axis=0))
    return tiles


def split2(x):
    one = x.astype(BF16)
    return one, (x - one.astype(F32)).astype(BF16)


def state_kernel(picks, core_ref, key_hbm, value_hbm, *refs):
    out_refs, (key, value, sems) = refs[: len(picks)], refs[len(picks) :]
    loads = []
    for n, (step, own) in enumerate(picks):
        half = core_ref[0] if own else 1 - core_ref[0]
        spot = pl.ds(pl.multiple_of(half * HALF, HALF), HALF)
        loads.append(
            (
                pltpu.make_async_copy(key_hbm.at[step, spot], key.at[n], sems.at[n, 0]),
                pltpu.make_async_copy(value_hbm.at[step, spot], value.at[n], sems.at[n, 1]),
            )
        )
    for pair in loads:
        for load in pair:
            load.start()
    for n, pair in enumerate(loads):
        for load in pair:
            load.wait()
        pack_states(key[n], value[n], out_refs[n])


def local_states(core, keys, values, picks):
    n = len(picks)
    hbm = pl.BlockSpec(memory_space=pltpu.HBM)
    return pl.pallas_call(
        functools.partial(state_kernel, picks),
        out_shape=(jax.ShapeDtypeStruct((PACKED, LANES), F32),) * n,
        in_specs=[pl.BlockSpec(memory_space=pltpu.SMEM), hbm, hbm],
        out_specs=(pl.BlockSpec(memory_space=pltpu.VMEM),) * n,
        scratch_shapes=[
            pltpu.VMEM((n, HALF, TOK), BF16),
            pltpu.VMEM((n, HALF, TOK), BF16),
            pltpu.SemaphoreType.DMA((n, 2)),
        ],
        compiler_params=pltpu.CompilerParams(vmem_limit_bytes=16 << 20),
        cost_estimate=pl.CostEstimate(flops=300_000_000 * n, bytes_accessed=800_000 * n, transcendentals=0),
        name="local_states",
    )(core, keys, values)


def convolve(padded, conv_weight):
    widened = jnp.pad(padded.astype(F32), ((0, 0), (1, 1), (0, 0)))
    summed = jnp.zeros((ROWS_DEV, COLS, padded.shape[-1]), F32)
    for tap_row in range(3):
        for tap_col in range(3):
            summed = (
                summed
                + widened[tap_row : tap_row + ROWS_DEV, tap_col : tap_col + COLS]
                * conv_weight[3 * tap_row + tap_col]
            )
    return summed.reshape(TOK, padded.shape[-1])


def mix_kernel(chunks, core_ref, step_ref, query_hbm, conv0_hbm, conv1_hbm, weight_hbm, gate_ref,
               own_ref, other_ref, keep0, send0, keep1, send1, out_hbm,
               query, acc, weight, mixed, result, sem_in, sem_out):
    loads = [
        pltpu.make_async_copy(query_hbm, query, sem_in.at[0]),
        pltpu.make_async_copy(conv0_hbm, acc.at[0], sem_in.at[1]),
        pltpu.make_async_copy(conv1_hbm, acc.at[1], sem_in.at[2]),
        pltpu.make_async_copy(weight_hbm, weight, sem_in.at[3]),
    ]
    for load in loads:
        load.start()
    gate_rows = [gate_ref[pl.ds(step_ref[s], 1), :] for s in range(2)]
    gates = jnp.concatenate(gate_rows + [gate_rows[0]] * 6, axis=0).T
    waited = False
    for part, (whole_ref, zero_ref, one_ref) in enumerate(((own_ref, keep0, keep1), (other_ref, send0, send1))):
        half = core_ref[0] if part == 0 else 1 - core_ref[0]
        base = half * HALF
        whole = whole_ref[...]
        states = (whole, whole - zero_ref[...] + one_ref[...])
        for step in range(2):
            tiles = unpack_tiles(states[step])
            if not waited:
                for load in loads[:3]:
                    load.wait()
                waited = True
            rows8 = lax.broadcasted_iota(jnp.int32, (HALF_HEADS, LANES), 0)
            rows = lax.broadcasted_iota(jnp.int32, (TROWS, LANES), 0)
            den = None
            sums = [None] * HALF_HEADS
            for tile, packed in enumerate(tiles):
                heads = [h for h in range(HALF_HEADS) if tile in tiles_of(h)]
                blocks = []
                for head in heads:
                    shift = HD * head % 8
                    block = jnp.where(lane_mask((TROWS, LANES), tile, head) & (rows < HD), packed, 0.0)
                    block = jnp.concatenate([block, jnp.zeros((SLAB - TROWS, LANES), F32)], axis=0)
                    if shift:
                        block = jnp.concatenate([block[SLAB - shift :], block[: SLAB - shift]], axis=0)
                    blocks.append(block)
                owner = jnp.zeros((HALF_HEADS, LANES), jnp.int32)
                for head in heads:
                    owner = jnp.where(lane_mask((HALF_HEADS, LANES), tile, head) & (rows8 == head), 1, owner)
                row = jnp.where(owner == 1, jnp.broadcast_to(packed[HD : HD + 1], (HALF_HEADS, LANES)), 0.0)
                blocks += [row, jnp.zeros((HALF_HEADS, LANES), F32)]
                left = jnp.concatenate(split2(jnp.concatenate(blocks, axis=0)), axis=1)
                q = query[step, pl.ds(pl.multiple_of(base + TILE_BASE[tile], 16), LANES)]
                got = jnp.dot(left, jnp.concatenate([q, q], axis=0), preferred_element_type=F32)
                for n, head in enumerate(heads):
                    part_sum = got[n * SLAB : (n + 1) * SLAB]
                    sums[head] = part_sum if sums[head] is None else sums[head] + part_sum
                part_den = got[len(heads) * SLAB : len(heads) * SLAB + HALF_HEADS]
                den = part_den if den is None else den + part_den
            inverse = 1.0 / den
            for head in range(HALF_HEADS):
                first = HD * head // 8 * 8
                count = -(-(HD * head - first + HD) // 8) * 8
                spot = pl.ds(pl.multiple_of(base + first, 8), count)
                acc[step, spot] = acc[step, spot] + sums[head][:count] * inverse[head : head + 1]
    for step in range(2):
        mixed[:, step * TOK : (step + 1) * TOK] = acc[step].astype(BF16)
    loads[3].wait()
    stores = []
    for n, (start, size) in enumerate(chunks):
        prod = lax.dot_general(
            weight[:, start : start + size], mixed[...], (((0,), (0,)), ((), ())), preferred_element_type=F32
        )
        for step in range(2):
            result[step, start : start + size] = (
                prod[:, step * TOK : (step + 1) * TOK] * gates[start : start + size, step : step + 1]
            )
            stores.append(
                pltpu.make_async_copy(
                    result.at[step, start : start + size], out_hbm.at[step, start : start + size], sem_out.at[n, step]
                )
            )
            stores[-1].start()
    for store in stores:
        store.wait()


def mix(core, timesteps, queries, conv, weight, gate_table, own, other, keep0, send0, keep1, send1):
    width = weight.shape[1]
    chunks = [(s, min(256, width - s)) for s in range(0, width, 256)]
    smem = pl.BlockSpec(memory_space=pltpu.SMEM)
    anyspace = pl.BlockSpec(memory_space=pl.ANY)
    vmem = pl.BlockSpec(memory_space=pltpu.VMEM)
    return pl.pallas_call(
        functools.partial(mix_kernel, chunks),
        out_shape=jax.ShapeDtypeStruct((2, width, TOK), F32),
        in_specs=[smem, smem, anyspace, anyspace, anyspace, anyspace] + [vmem] * 7,
        out_specs=anyspace,
        scratch_shapes=[
            pltpu.VMEM((2, 2 * HALF, TOK), BF16),
            pltpu.VMEM((2, 2 * HALF, TOK), F32),
            pltpu.VMEM((2 * HALF, width), BF16),
            pltpu.VMEM((2 * HALF, 2 * TOK), BF16),
            pltpu.VMEM((2, width, TOK), F32),
            pltpu.SemaphoreType.DMA((4,)),
            pltpu.SemaphoreType.DMA((len(chunks), 2)),
        ],
        compiler_params=pltpu.CompilerParams(vmem_limit_bytes=LIMIT),
        cost_estimate=pl.CostEstimate(flops=3_000_000_000, bytes_accessed=14_000_000, transcendentals=0),
        name="mix",
    )(core, timesteps, queries, *conv, weight, gate_table, own, other, keep0, send0, keep1, send1)


def fresh_kernel(scale, core_ref, own_ref, other_ref, state_ref, total_ref):
    first = core_ref[0] == 0
    own, other = own_ref[...], other_ref[...]
    halves = (jnp.where(first, own, other), jnp.where(first, other, own))
    lanes = lax.broadcasted_iota(jnp.int32, (TROWS, LANES), 1)
    for half, packed in enumerate(halves):
        tiles = unpack_tiles(packed * scale)
        for head in range(HALF_HEADS):
            block = None
            for tile in tiles_of(head):
                low = max(HD * head, LANES * tile)
                turn = (HD * head - TILE_BASE[tile]) % LANES
                moved = pltpu.roll(tiles[tile], (LANES - turn) % LANES, 1) if turn else tiles[tile]
                block = moved if block is None else jnp.where(lanes >= low - HD * head, moved, block)
            at = half * HALF_HEADS + head
            total_ref[at : at + 1, :] = block[HD : HD + 1, :HD]
            state_ref[:, at, :] = block.T[:HD, :HD]


def fresh(core, own, other, tokens):
    return pl.pallas_call(
        functools.partial(fresh_kernel, 1.0 / tokens),
        out_shape=(jax.ShapeDtypeStruct((HD, NH, HD), F32), jax.ShapeDtypeStruct((NH, HD), F32)),
        in_specs=[pl.BlockSpec(memory_space=pltpu.SMEM)] + [pl.BlockSpec(memory_space=pltpu.VMEM)] * 2,
        out_specs=(pl.BlockSpec(memory_space=pltpu.VMEM),) * 2,
        compiler_params=pltpu.CompilerParams(vmem_limit_bytes=LIMIT),
        name="fresh",
    )(core, own, other)


def local(queries, keys, values, timesteps, gate_table, out_weight, conv_weight):
    count = lax.axis_size("tm")
    tokens = queries.shape[1] * count
    core = (lax.axis_index("tm") % 2).astype(jnp.int32).reshape(1)
    plain = with_layout_constraint(values, Layout((0, 1, 2)))
    grid = plain.reshape(2, ROWS_DEV, COLS, values.shape[-1])
    queries, keys, values = (
        pltpu.with_memory_space_constraint(x.transpose(0, 2, 1), pltpu.HBM) for x in (queries, keys, values)
    )

    def swap(x, pick):
        return lax.ppermute(x, "tm", [(i, i ^ pick(i % 2)) for i in range(count)])

    def partner(x):
        return swap(x, lambda c: 1)

    bits = [1 << b for b in range(1, count.bit_length() - 1)]
    turned = bits[-1:] + bits[:-1]
    rounds = [lambda c, b=b, t=t: t if c else b for b, t in zip(bits, turned)]

    first = core[0] == 0
    (send0,) = local_states(core, keys, values, ((0, 0),))
    (keep0,) = local_states(core, keys, values, ((0, 1),))
    send1, keep1 = local_states(core, keys, values, ((1, 0), (1, 1)))
    near = jnp.where(first, grid[0, -1], grid[0, 0])
    far = jnp.where(first, grid[0, 0], grid[0, -1])
    near = partner(near)
    links = [p for i in range(1, count - 1, 2) for p in ((i, i + 1), (i + 1, i))]
    far = lax.ppermute(far, "tm", links)
    above, below = jnp.where(first, far, near), jnp.where(first, near, far)
    conv = [
        convolve(jnp.concatenate([above[None], grid[s], below[None]], axis=0), conv_weight).T for s in range(2)
    ]
    got0 = partner(send0)
    got1 = partner(send1)
    whole, second = keep0 + got0, keep1 + got1
    for pick in rounds:
        got = swap(whole, pick)
        whole = whole + got
    for pick in rounds[1:] + rounds[:1]:
        got = swap(second, pick)
        second = second + got
    other = partner(whole)
    update = mix(core, timesteps, queries, conv, out_weight, gate_table, whole, other, keep0, send0, keep1, send1)
    other1 = partner(second)
    fresh_state, fresh_total = fresh(core, second, other1, tokens)
    return update.transpose(0, 2, 1), fresh_state.transpose(1, 0, 2), fresh_total


def solution(mesh):
    placed = (
        P(None, ("grp", "tm"), None),
        P(None, ("grp", "tm"), None),
        P(None, ("grp", "tm"), None),
        P("grp"),
        P(),
        P(),
        P(),
    )

    return jax.shard_map(
        local,
        mesh=mesh,
        in_specs=placed,
        out_specs=(P(None, ("grp", "tm"), None), P("grp", None, None), P("grp", None)),
        check_vma=False,
    )
```

```python
import functools

import jax
import jax.numpy as jnp
from jax import lax
from jax.experimental import pallas as pl
from jax.experimental.pallas import tpu as pltpu
from jax.sharding import PartitionSpec as P


NH = 16
HD = 70
COLS = 64
ROWS_DEV = 4

F32 = jnp.float32
BF16 = jnp.bfloat16
LANES = 128
HALF_HEADS = NH // 2
HALF = HALF_HEADS * HD
TOK = ROWS_DEV * COLS
FULL_TILES = HALF // LANES
TILE_BASE = [LANES * j for j in range(FULL_TILES)] + [HALF - LANES]
REST = HALF - LANES * FULL_TILES
TROWS = 72
FOLD = 40
SLAB = 80
PACKED = FULL_TILES * TROWS + FOLD
LIMIT = 24 << 20


def core_of():
    return lax.rem(lax.axis_index("tm"), 2)


def tiles_of(head):
    first, last = HD * head, HD * head + HD
    return [j for j in range(FULL_TILES + 1) if first < min(LANES * j + LANES, HALF) and last > LANES * j]


def lane_mask(shape, tile, head):
    chan = TILE_BASE[tile] + lax.broadcasted_iota(jnp.int32, shape, 1)
    low = max(HD * head, LANES * tile)
    return (chan >= low) & (chan < HD * head + HD)


def nt_dot(a, b):
    return lax.dot_general(a, b, (((1,), (1,)), ((), ())), preferred_element_type=F32)


def pack_states(keys, values, out_ref):
    acc = [jnp.zeros((TROWS, LANES), F32) for _ in TILE_BASE]
    rows = lax.broadcasted_iota(jnp.int32, (TROWS, LANES), 0)
    for head in range(HALF_HEADS):
        start = HD * head // 16 * 16
        stop = min(HALF, -(-(HD * head + HD) // 16) * 16)
        shift = HD * head - start
        for tile in tiles_of(head):
            base = TILE_BASE[tile]
            prod = nt_dot(values[start:stop], keys[base : base + LANES])
            part = jnp.concatenate([prod[shift : shift + HD], jnp.zeros((TROWS - HD, LANES), F32)], axis=0)
            acc[tile] = jnp.where(lane_mask((TROWS, LANES), tile, head), part, acc[tile])
    ones = jnp.ones((16, TOK), BF16)
    for tile, base in enumerate(TILE_BASE):
        total = nt_dot(ones, keys[base : base + LANES])[:1]
        acc[tile] = jnp.where(rows == HD, jnp.broadcast_to(total, (TROWS, LANES)), acc[tile])
    for tile in range(FULL_TILES):
        out_ref[tile * TROWS : (tile + 1) * TROWS] = acc[tile]
    last = acc[FULL_TILES]
    low = jnp.concatenate([last[FOLD:], jnp.zeros((2 * FOLD - TROWS, LANES), F32)], axis=0)
    lanes = lax.broadcasted_iota(jnp.int32, (FOLD, LANES), 1)
    out_ref[FULL_TILES * TROWS :] = jnp.where(lanes >= LANES - REST, last[:FOLD], pltpu.roll(low, LANES // 2, 1))


def unpack_tiles(packed):
    tiles = [packed[j * TROWS : (j + 1) * TROWS] for j in range(FULL_TILES)]
    fold = packed[FULL_TILES * TROWS :]
    tiles.append(jnp.concatenate([fold, pltpu.roll(fold, LANES // 2, 1)[: TROWS - FOLD]], axis=0))
    return tiles


def split2(x):
    one = x.astype(BF16)
    return one, (x - one.astype(F32)).astype(BF16)


def state_kernel(picks, key_hbm, value_hbm, *refs):
    out_refs, (key, value, sems) = refs[: len(picks)], refs[len(picks) :]
    loads = []
    for n, (step, own) in enumerate(picks):
        half = core_of() if own else 1 - core_of()
        spot = pl.ds(pl.multiple_of(half * HALF, HALF), HALF)
        loads.append(
            (
                pltpu.make_async_copy(key_hbm.at[step, spot], key.at[n], sems.at[n, 0]),
                pltpu.make_async_copy(value_hbm.at[step, spot], value.at[n], sems.at[n, 1]),
            )
        )
    for pair in loads:
        for load in pair:
            load.start()
    for n, pair in enumerate(loads):
        for load in pair:
            load.wait()
        pack_states(key[n], value[n], out_refs[n])


def held_kernel(picks, key_ref, value_ref, *out_refs):
    for (step, own), out_ref in zip(picks, out_refs):
        half = core_of() if own else 1 - core_of()
        spot = pl.ds(pl.multiple_of(half * HALF, HALF), HALF)
        pack_states(key_ref[step, spot], value_ref[step, spot], out_ref)


def held_states(keys, values, picks):
    n = len(picks)
    vmem = pl.BlockSpec(memory_space=pltpu.VMEM)
    return pl.pallas_call(
        functools.partial(held_kernel, picks),
        out_shape=(jax.ShapeDtypeStruct((PACKED, LANES), F32),) * n,
        in_specs=[vmem, vmem],
        out_specs=(vmem,) * n,
        compiler_params=pltpu.CompilerParams(vmem_limit_bytes=8 << 20),
        cost_estimate=pl.CostEstimate(flops=300_000_000 * n, bytes_accessed=800_000 * n, transcendentals=0),
        name="held_states",
    )(keys, values)


def local_states(keys, values, picks):
    n = len(picks)
    hbm = pl.BlockSpec(memory_space=pltpu.HBM)
    return pl.pallas_call(
        functools.partial(state_kernel, picks),
        out_shape=(jax.ShapeDtypeStruct((PACKED, LANES), F32),) * n,
        in_specs=[hbm, hbm],
        out_specs=(pl.BlockSpec(memory_space=pltpu.VMEM),) * n,
        scratch_shapes=[
            pltpu.VMEM((n, HALF, TOK), BF16),
            pltpu.VMEM((n, HALF, TOK), BF16),
            pltpu.SemaphoreType.DMA((n, 2)),
        ],
        compiler_params=pltpu.CompilerParams(vmem_limit_bytes=4 << 20),
        cost_estimate=pl.CostEstimate(flops=300_000_000 * n, bytes_accessed=800_000 * n, transcendentals=0),
        name="local_states",
    )(keys, values)


def plain_kernel(value_ref, plain_ref, near_ref, far_ref):
    first = core_of() == 0
    for step in range(2):
        plain_ref[step] = value_ref[step].T
    head, tail = plain_ref[0, :COLS], plain_ref[0, TOK - COLS :]
    near_ref[...] = jnp.where(first, tail, head)
    far_ref[...] = jnp.where(first, head, tail)


def plain_values(values):
    vmem = pl.BlockSpec(memory_space=pltpu.VMEM)
    width = values.shape[1]
    row = jax.ShapeDtypeStruct((COLS, width), BF16)
    return pl.pallas_call(
        plain_kernel,
        out_shape=(jax.ShapeDtypeStruct((2, TOK, width), BF16), row, row),
        in_specs=[vmem],
        out_specs=(vmem,) * 3,
        compiler_params=pltpu.CompilerParams(vmem_limit_bytes=8 << 20),
        cost_estimate=pl.CostEstimate(flops=1_000_000, bytes_accessed=2_400_000, transcendentals=0),
        name="plain_values",
    )(values)


def convolve(padded, conv_weight):
    widened = jnp.pad(padded.astype(F32), ((0, 0), (1, 1), (0, 0)))
    summed = jnp.zeros((ROWS_DEV, COLS, padded.shape[-1]), F32)
    for tap_row in range(3):
        for tap_col in range(3):
            summed = (
                summed
                + widened[tap_row : tap_row + ROWS_DEV, tap_col : tap_col + COLS]
                * conv_weight[3 * tap_row + tap_col]
            )
    return summed.reshape(TOK, padded.shape[-1])


def spread_kernel(own, query, whole_ref, zero_ref, one_ref, out_ref):
    half = core_of() if own else 1 - core_of()
    base = half * HALF
    whole = whole_ref[...]
    states = (whole, whole - zero_ref[...] + one_ref[...])
    rows8 = lax.broadcasted_iota(jnp.int32, (HALF_HEADS, LANES), 0)
    rows = lax.broadcasted_iota(jnp.int32, (TROWS, LANES), 0)
    for step in range(2):
        tiles = unpack_tiles(states[step])
        den = None
        sums = [None] * HALF_HEADS
        for tile, packed in enumerate(tiles):
            heads = [h for h in range(HALF_HEADS) if tile in tiles_of(h)]
            blocks = []
            for head in heads:
                shift = HD * head % 8
                block = jnp.where(lane_mask((TROWS, LANES), tile, head) & (rows < HD), packed, 0.0)
                block = jnp.concatenate([block, jnp.zeros((SLAB - TROWS, LANES), F32)], axis=0)
                if shift:
                    block = jnp.concatenate([block[SLAB - shift :], block[: SLAB - shift]], axis=0)
                blocks.append(block)
            owner = jnp.zeros((HALF_HEADS, LANES), jnp.int32)
            for head in heads:
                owner = jnp.where(lane_mask((HALF_HEADS, LANES), tile, head) & (rows8 == head), 1, owner)
            row = jnp.where(owner == 1, jnp.broadcast_to(packed[HD : HD + 1], (HALF_HEADS, LANES)), 0.0)
            blocks += [row, jnp.zeros((HALF_HEADS, LANES), F32)]
            left = jnp.concatenate(split2(jnp.concatenate(blocks, axis=0)), axis=1)
            q = query[step, pl.ds(pl.multiple_of(base + TILE_BASE[tile], 16), LANES)]
            got = jnp.dot(left, jnp.concatenate([q, q], axis=0), preferred_element_type=F32)
            for n, head in enumerate(heads):
                part_sum = got[n * SLAB : (n + 1) * SLAB]
                sums[head] = part_sum if sums[head] is None else sums[head] + part_sum
            part_den = got[len(heads) * SLAB : len(heads) * SLAB + HALF_HEADS]
            den = part_den if den is None else den + part_den
        inverse = 1.0 / den
        out_ref[step] = jnp.zeros((HALF, TOK), F32)
        for head in range(HALF_HEADS):
            first = HD * head // 8 * 8
            count = -(-(HD * head - first + HD) // 8) * 8
            spot = slice(first, first + count)
            out_ref[step, spot] = out_ref[step, spot] + sums[head][:count] * inverse[head : head + 1]


def spread(own, queries, whole, zero, one):
    vmem = pl.BlockSpec(memory_space=pltpu.VMEM)
    return pl.pallas_call(
        functools.partial(spread_kernel, own),
        out_shape=jax.ShapeDtypeStruct((2, HALF, TOK), F32),
        in_specs=[vmem] * 4,
        out_specs=vmem,
        compiler_params=pltpu.CompilerParams(vmem_limit_bytes=8 << 20),
        cost_estimate=pl.CostEstimate(flops=800_000_000, bytes_accessed=2_000_000, transcendentals=0),
        name="spread",
    )(queries, whole, zero, one)


def project_kernel(chunks, step_ref, conv0, conv1, weight_hbm, gate_ref, own_ref, other_ref, out_hbm,
                   weight, turned, mixed, result, sem_in, sem_out):
    load = pltpu.make_async_copy(weight_hbm, weight, sem_in)
    load.start()
    half = core_of()
    for step in range(2):
        turned[...] = (conv0, conv1)[step][...].T
        for at, part in ((half, own_ref), (1 - half, other_ref)):
            spot = pl.ds(pl.multiple_of(at * HALF, HALF), HALF)
            mixed[spot, step * TOK : (step + 1) * TOK] = (part[step] + turned[spot]).astype(BF16)
    gate_rows = [gate_ref[pl.ds(step_ref[s], 1), :] for s in range(2)]
    gates = jnp.concatenate(gate_rows + [gate_rows[0]] * 6, axis=0).T
    load.wait()
    stores = []
    for n, (start, size) in enumerate(chunks):
        prod = lax.dot_general(
            weight[:, start : start + size], mixed[...], (((0,), (0,)), ((), ())), preferred_element_type=F32
        )
        for step in range(2):
            result[step, start : start + size] = (
                prod[:, step * TOK : (step + 1) * TOK] * gates[start : start + size, step : step + 1]
            )
            stores.append(
                pltpu.make_async_copy(
                    result.at[step, start : start + size], out_hbm.at[step, start : start + size], sem_out.at[n, step]
                )
            )
            stores[-1].start()
    for store in stores:
        store.wait()


def project(timesteps, conv, weight, gate_table, own, other):
    width = weight.shape[1]
    chunks = [(s, min(256, width - s)) for s in range(0, width, 256)]
    vmem = pl.BlockSpec(memory_space=pltpu.VMEM)
    anyspace = pl.BlockSpec(memory_space=pl.ANY)
    return pl.pallas_call(
        functools.partial(project_kernel, chunks),
        out_shape=jax.ShapeDtypeStruct((2, width, TOK), F32),
        in_specs=[pl.BlockSpec(memory_space=pltpu.SMEM), vmem, vmem, anyspace, vmem, vmem, vmem],
        out_specs=anyspace,
        scratch_shapes=[
            pltpu.VMEM((2 * HALF, width), BF16),
            pltpu.VMEM((2 * HALF, TOK), F32),
            pltpu.VMEM((2 * HALF, 2 * TOK), BF16),
            pltpu.VMEM((2, width, TOK), F32),
            pltpu.SemaphoreType.DMA,
            pltpu.SemaphoreType.DMA((len(chunks), 2)),
        ],
        compiler_params=pltpu.CompilerParams(vmem_limit_bytes=LIMIT),
        cost_estimate=pl.CostEstimate(flops=3_000_000_000, bytes_accessed=14_000_000, transcendentals=0),
        name="project",
    )(timesteps, *conv, weight, gate_table, own, other)


def fresh_kernel(scale, own_ref, other_ref, state_ref, total_ref):
    first = core_of() == 0
    own, other = own_ref[...], other_ref[...]
    halves = (jnp.where(first, own, other), jnp.where(first, other, own))
    lanes = lax.broadcasted_iota(jnp.int32, (TROWS, LANES), 1)
    for half, packed in enumerate(halves):
        tiles = unpack_tiles(packed * scale)
        for head in range(HALF_HEADS):
            block = None
            for tile in tiles_of(head):
                low = max(HD * head, LANES * tile)
                turn = (HD * head - TILE_BASE[tile]) % LANES
                moved = pltpu.roll(tiles[tile], (LANES - turn) % LANES, 1) if turn else tiles[tile]
                block = moved if block is None else jnp.where(lanes >= low - HD * head, moved, block)
            at = half * HALF_HEADS + head
            total_ref[at : at + 1, :] = block[HD : HD + 1, :HD]
            state_ref[:, at, :] = block.T[:HD, :HD]


def fresh(own, other, tokens):
    return pl.pallas_call(
        functools.partial(fresh_kernel, 1.0 / tokens),
        out_shape=(jax.ShapeDtypeStruct((HD, NH, HD), F32), jax.ShapeDtypeStruct((NH, HD), F32)),
        in_specs=[pl.BlockSpec(memory_space=pltpu.VMEM)] * 2,
        out_specs=(pl.BlockSpec(memory_space=pltpu.VMEM),) * 2,
        compiler_params=pltpu.CompilerParams(vmem_limit_bytes=LIMIT),
        name="fresh",
    )(own, other)


def local(queries, keys, values, timesteps, gate_table, out_weight, conv_weight):
    count = lax.axis_size("tm")
    tokens = queries.shape[1] * count
    queries, keys, values = (x.transpose(0, 2, 1) for x in (queries, keys, values))
    far_keys, far_values = (pltpu.with_memory_space_constraint(x, pltpu.HBM) for x in (keys, values))

    def swap(x, pick):
        return lax.ppermute(x, "tm", [(i, i ^ pick(i % 2)) for i in range(count)])

    def partner(x):
        return swap(x, lambda c: 1)

    bits = [1 << b for b in range(1, count.bit_length() - 1)]
    turned = bits[-1:] + bits[:-1]
    rounds = [lambda c, b=b, t=t: t if c else b for b, t in zip(bits, turned)]

    first = core_of() == 0
    (send0,) = local_states(far_keys, far_values, ((0, 0),))
    (keep0,) = held_states(keys, values, ((0, 1),))
    send1, keep1 = held_states(keys, values, ((1, 0), (1, 1)))
    plain, near, far = plain_values(values)
    near = partner(near)
    links = [p for i in range(1, count - 1, 2) for p in ((i, i + 1), (i + 1, i))]
    far = lax.ppermute(far, "tm", links)
    above, below = jnp.where(first, far, near), jnp.where(first, near, far)
    grid = plain.reshape(2, ROWS_DEV, COLS, plain.shape[-1])
    conv0 = convolve(jnp.concatenate([above[None], grid[0], below[None]], axis=0), conv_weight)
    again, above, below, weights, conv0 = lax.optimization_barrier((grid[1], above, below, conv_weight, conv0))
    conv1 = convolve(jnp.concatenate([above[None], again, below[None]], axis=0), weights)
    conv = conv0, conv1
    got0 = partner(send0)
    got1 = partner(send1)
    whole, second = keep0 + got0, keep1 + got1
    for pick in rounds:
        got = swap(whole, pick)
        whole = whole + got
    for pick in rounds[1:] + rounds[:1]:
        got = swap(second, pick)
        second = second + got
    other = partner(whole)
    own = spread(True, queries, whole, keep0, keep1)
    rest = spread(False, queries, other, send0, send1)
    update = project(timesteps, conv, out_weight, gate_table, own, rest)
    other1 = partner(second)
    fresh_state, fresh_total = fresh(second, other1, tokens)
    return update.transpose(0, 2, 1), fresh_state.transpose(1, 0, 2), fresh_total


def solution(mesh):
    placed = (
        P(None, ("grp", "tm"), None),
        P(None, ("grp", "tm"), None),
        P(None, ("grp", "tm"), None),
        P("grp"),
        P(),
        P(),
        P(),
    )

    return jax.shard_map(
        local,
        mesh=mesh,
        in_specs=placed,
        out_specs=(P(None, ("grp", "tm"), None), P("grp", None, None), P("grp", None)),
        check_vma=False,
    )
```

```python
import functools

import jax
import jax.numpy as jnp
from jax import lax
from jax.experimental import pallas as pl
from jax.experimental.pallas import tpu as pltpu
from jax.sharding import PartitionSpec as P


NH = 16
HD = 70
COLS = 64
ROWS_DEV = 4

F32 = jnp.float32
BF16 = jnp.bfloat16
LANES = 128
HALF_HEADS = NH // 2
HALF = HALF_HEADS * HD
TOK = ROWS_DEV * COLS
FULL_TILES = HALF // LANES
TILE_BASE = [LANES * j for j in range(FULL_TILES)] + [HALF - LANES]
REST = HALF - LANES * FULL_TILES
TROWS = 72
FOLD = 40
SLAB = 80
FIRST_ORDERS = (0, 1, 2), (1, 2, 0)
SECOND_ORDERS = (2, 0, 1), (0, 1, 2)
PACKED = FULL_TILES * TROWS + FOLD
LIMIT = 16 << 20


def core_of():
    return lax.rem(lax.axis_index("tm"), 2)


def tiles_of(head):
    first, last = HD * head, HD * head + HD
    return [j for j in range(FULL_TILES + 1) if first < min(LANES * j + LANES, HALF) and last > LANES * j]


def lane_mask(shape, tile, head):
    chan = TILE_BASE[tile] + lax.broadcasted_iota(jnp.int32, shape, 1)
    low = max(HD * head, LANES * tile)
    return (chan >= low) & (chan < HD * head + HD)


def nt_dot(a, b):
    return lax.dot_general(a, b, (((1,), (1,)), ((), ())), preferred_element_type=F32)


def pack_states(keys, values, out_ref):
    acc = [jnp.zeros((TROWS, LANES), F32) for _ in TILE_BASE]
    rows = lax.broadcasted_iota(jnp.int32, (TROWS, LANES), 0)
    for head in range(HALF_HEADS):
        start = HD * head // 16 * 16
        stop = min(HALF, -(-(HD * head + HD) // 16) * 16)
        shift = HD * head - start
        for tile in tiles_of(head):
            base = TILE_BASE[tile]
            prod = nt_dot(values[start:stop], keys[base : base + LANES])
            part = jnp.concatenate([prod[shift : shift + HD], jnp.zeros((TROWS - HD, LANES), F32)], axis=0)
            acc[tile] = jnp.where(lane_mask((TROWS, LANES), tile, head), part, acc[tile])
    ones = jnp.ones((16, TOK), BF16)
    for tile, base in enumerate(TILE_BASE):
        total = nt_dot(ones, keys[base : base + LANES])[:1]
        acc[tile] = jnp.where(rows == HD, jnp.broadcast_to(total, (TROWS, LANES)), acc[tile])
    for tile in range(FULL_TILES):
        out_ref[tile * TROWS : (tile + 1) * TROWS] = acc[tile]
    last = acc[FULL_TILES]
    low = jnp.concatenate([last[FOLD:], jnp.zeros((2 * FOLD - TROWS, LANES), F32)], axis=0)
    lanes = lax.broadcasted_iota(jnp.int32, (FOLD, LANES), 1)
    out_ref[FULL_TILES * TROWS :] = jnp.where(lanes >= LANES - REST, last[:FOLD], pltpu.roll(low, LANES // 2, 1))


def unpack_tiles(packed):
    tiles = [packed[j * TROWS : (j + 1) * TROWS] for j in range(FULL_TILES)]
    fold = packed[FULL_TILES * TROWS :]
    tiles.append(jnp.concatenate([fold, pltpu.roll(fold, LANES // 2, 1)[: TROWS - FOLD]], axis=0))
    return tiles


def split2(x):
    one = x.astype(BF16)
    return one, (x - one.astype(F32)).astype(BF16)


def state_kernel(picks, key_hbm, value_hbm, *refs):
    out_refs, (key, value, sems) = refs[: len(picks)], refs[len(picks) :]
    loads = []
    for n, (step, own) in enumerate(picks):
        half = core_of() if own else 1 - core_of()
        spot = pl.ds(pl.multiple_of(half * HALF, HALF), HALF)
        loads.append(
            (
                pltpu.make_async_copy(key_hbm.at[step, spot], key.at[n], sems.at[n, 0]),
                pltpu.make_async_copy(value_hbm.at[step, spot], value.at[n], sems.at[n, 1]),
            )
        )
    for pair in loads:
        for load in pair:
            load.start()
    for n, pair in enumerate(loads):
        for load in pair:
            load.wait()
        pack_states(key[n], value[n], out_refs[n])


def held_kernel(picks, key_ref, value_ref, *out_refs):
    for (step, own), out_ref in zip(picks, out_refs):
        half = core_of() if own else 1 - core_of()
        spot = pl.ds(pl.multiple_of(half * HALF, HALF), HALF)
        pack_states(key_ref[step, spot], value_ref[step, spot], out_ref)


def held_states(keys, values, picks):
    n = len(picks)
    vmem = pl.BlockSpec(memory_space=pltpu.VMEM)
    return pl.pallas_call(
        functools.partial(held_kernel, picks),
        out_shape=(jax.ShapeDtypeStruct((PACKED, LANES), F32),) * n,
        in_specs=[vmem, vmem],
        out_specs=(vmem,) * n,
        compiler_params=pltpu.CompilerParams(vmem_limit_bytes=8 << 20),
        cost_estimate=pl.CostEstimate(flops=300_000_000 * n, bytes_accessed=800_000 * n, transcendentals=0),
        name="held_states",
    )(keys, values)


def local_states(keys, values, picks):
    n = len(picks)
    hbm = pl.BlockSpec(memory_space=pltpu.HBM)
    return pl.pallas_call(
        functools.partial(state_kernel, picks),
        out_shape=(jax.ShapeDtypeStruct((PACKED, LANES), F32),) * n,
        in_specs=[hbm, hbm],
        out_specs=(pl.BlockSpec(memory_space=pltpu.VMEM),) * n,
        scratch_shapes=[
            pltpu.VMEM((n, HALF, TOK), BF16),
            pltpu.VMEM((n, HALF, TOK), BF16),
            pltpu.SemaphoreType.DMA((n, 2)),
        ],
        compiler_params=pltpu.CompilerParams(vmem_limit_bytes=4 << 20),
        cost_estimate=pl.CostEstimate(flops=300_000_000 * n, bytes_accessed=800_000 * n, transcendentals=0),
        name="local_states",
    )(keys, values)


def plain_kernel(value_ref, weight_ref, plain_ref, near_ref, far_ref, taps_ref):
    taps_ref[...] = weight_ref[...]
    first = core_of() == 0
    for step in range(2):
        plain_ref[step] = value_ref[step].T
    head, tail = plain_ref[0, :COLS], plain_ref[0, TOK - COLS :]
    near_ref[...] = jnp.where(first, tail, head)
    far_ref[...] = jnp.where(first, head, tail)


def plain_values(values, weights):
    vmem = pl.BlockSpec(memory_space=pltpu.VMEM)
    width = values.shape[1]
    row = jax.ShapeDtypeStruct((COLS, width), BF16)
    return pl.pallas_call(
        plain_kernel,
        out_shape=(jax.ShapeDtypeStruct((2, TOK, width), BF16), row, row, jax.ShapeDtypeStruct(weights.shape, F32)),
        in_specs=[vmem] * 2,
        out_specs=(vmem,) * 4,
        compiler_params=pltpu.CompilerParams(vmem_limit_bytes=8 << 20),
        cost_estimate=pl.CostEstimate(flops=1_000_000, bytes_accessed=2_400_000, transcendentals=0),
        name="plain_values",
    )(values, weights)


def convolve(padded, conv_weight):
    widened = jnp.pad(padded.astype(F32), ((0, 0), (1, 1), (0, 0)))
    summed = jnp.zeros((ROWS_DEV, COLS, padded.shape[-1]), F32)
    for tap_row in range(3):
        for tap_col in range(3):
            summed = (
                summed
                + widened[tap_row : tap_row + ROWS_DEV, tap_col : tap_col + COLS]
                * conv_weight[3 * tap_row + tap_col]
            )
    return summed.reshape(TOK, padded.shape[-1])


def spread_kernel(own, query, conv_ref, whole_ref, zero_ref, one_ref, out_ref, acc):
    half = core_of() if own else 1 - core_of()
    base = half * HALF
    whole = whole_ref[...]
    states = (whole, whole - zero_ref[...] + one_ref[...])
    rows8 = lax.broadcasted_iota(jnp.int32, (HALF_HEADS, LANES), 0)
    rows = lax.broadcasted_iota(jnp.int32, (TROWS, LANES), 0)
    for step in range(2):
        tiles = unpack_tiles(states[step])
        den = None
        sums = [None] * HALF_HEADS
        for tile, packed in enumerate(tiles):
            heads = [h for h in range(HALF_HEADS) if tile in tiles_of(h)]
            blocks = []
            for head in heads:
                shift = HD * head % 8
                block = jnp.where(lane_mask((TROWS, LANES), tile, head) & (rows < HD), packed, 0.0)
                block = jnp.concatenate([block, jnp.zeros((SLAB - TROWS, LANES), F32)], axis=0)
                if shift:
                    block = jnp.concatenate([block[SLAB - shift :], block[: SLAB - shift]], axis=0)
                blocks.append(block)
            owner = jnp.zeros((HALF_HEADS, LANES), jnp.int32)
            for head in heads:
                owner = jnp.where(lane_mask((HALF_HEADS, LANES), tile, head) & (rows8 == head), 1, owner)
            row = jnp.where(owner == 1, jnp.broadcast_to(packed[HD : HD + 1], (HALF_HEADS, LANES)), 0.0)
            blocks += [row, jnp.zeros((HALF_HEADS, LANES), F32)]
            left = jnp.concatenate(split2(jnp.concatenate(blocks, axis=0)), axis=1)
            q = query[step, pl.ds(pl.multiple_of(base + TILE_BASE[tile], 16), LANES)]
            got = jnp.dot(left, jnp.concatenate([q, q], axis=0), preferred_element_type=F32)
            for n, head in enumerate(heads):
                part_sum = got[n * SLAB : (n + 1) * SLAB]
                sums[head] = part_sum if sums[head] is None else sums[head] + part_sum
            part_den = got[len(heads) * SLAB : len(heads) * SLAB + HALF_HEADS]
            den = part_den if den is None else den + part_den
        inverse = 1.0 / den
        acc[...] = jnp.zeros((HALF, TOK), F32)
        for head in range(HALF_HEADS):
            first = HD * head // 8 * 8
            count = -(-(HD * head - first + HD) // 8) * 8
            spot = slice(first, first + count)
            acc[spot] = acc[spot] + sums[head][:count] * inverse[head : head + 1]
        conv = conv_ref[step, pl.ds(pl.multiple_of(base, HALF), HALF)]
        out_ref[:, step * TOK : (step + 1) * TOK] = (acc[...] + conv).astype(BF16)


def spread(own, queries, conv, whole, zero, one):
    vmem = pl.BlockSpec(memory_space=pltpu.VMEM)
    return pl.pallas_call(
        functools.partial(spread_kernel, own),
        out_shape=jax.ShapeDtypeStruct((HALF, 2 * TOK), BF16),
        in_specs=[vmem] * 5,
        out_specs=vmem,
        scratch_shapes=[pltpu.VMEM((HALF, TOK), F32)],
        compiler_params=pltpu.CompilerParams(vmem_limit_bytes=8 << 20),
        cost_estimate=pl.CostEstimate(flops=800_000_000, bytes_accessed=2_000_000, transcendentals=0),
        name="spread",
    )(queries, conv, whole, zero, one)


def turn_kernel(conv0, conv1, out_ref):
    for step, conv in enumerate((conv0, conv1)):
        out_ref[step] = conv[...].T


def turn(conv0, conv1):
    tokens, width = conv0.shape
    vmem = pl.BlockSpec(memory_space=pltpu.VMEM)
    return pl.pallas_call(
        turn_kernel,
        out_shape=jax.ShapeDtypeStruct((2, width, tokens), F32),
        in_specs=[vmem] * 2,
        out_specs=vmem,
        compiler_params=pltpu.CompilerParams(vmem_limit_bytes=8 << 20),
        cost_estimate=pl.CostEstimate(flops=1_000_000, bytes_accessed=4_600_000, transcendentals=0),
        name="turn",
    )(conv0, conv1)


def project_kernel(chunks, step_ref, weight, gate_ref, own_ref, other_ref, out_hbm, mixed, result, sem_out):
    half = core_of()
    for at, part in ((half, own_ref), (1 - half, other_ref)):
        mixed[pl.ds(pl.multiple_of(at * HALF, HALF), HALF)] = part[...]
    gate_rows = [gate_ref[pl.ds(step_ref[s], 1), :] for s in range(2)]
    gates = jnp.concatenate(gate_rows + [gate_rows[0]] * 6, axis=0).T
    stores = []
    for n, (start, size) in enumerate(chunks):
        prod = lax.dot_general(
            weight[:, start : start + size], mixed[...], (((0,), (0,)), ((), ())), preferred_element_type=F32
        )
        for step in range(2):
            result[step, start : start + size] = (
                prod[:, step * TOK : (step + 1) * TOK] * gates[start : start + size, step : step + 1]
            )
            stores.append(
                pltpu.make_async_copy(
                    result.at[step, start : start + size], out_hbm.at[step, start : start + size], sem_out.at[n, step]
                )
            )
            stores[-1].start()
    for store in stores:
        store.wait()


def stage_kernel(weight_hbm, out_ref, sem):
    load = pltpu.make_async_copy(weight_hbm, out_ref, sem)
    load.start()
    load.wait()


def stage(weight):
    return pl.pallas_call(
        stage_kernel,
        out_shape=jax.ShapeDtypeStruct(weight.shape, weight.dtype),
        in_specs=[pl.BlockSpec(memory_space=pltpu.HBM)],
        out_specs=pl.BlockSpec(memory_space=pltpu.VMEM),
        scratch_shapes=[pltpu.SemaphoreType.DMA],
        compiler_params=pltpu.CompilerParams(vmem_limit_bytes=8 << 20),
        cost_estimate=pl.CostEstimate(flops=0, bytes_accessed=5_000_000, transcendentals=0),
        name="stage",
    )(weight)


def project(timesteps, weight, gate_table, own, other):
    width = weight.shape[1]
    chunks = [(s, min(256, width - s)) for s in range(0, width, 256)]
    vmem = pl.BlockSpec(memory_space=pltpu.VMEM)
    anyspace = pl.BlockSpec(memory_space=pl.ANY)
    return pl.pallas_call(
        functools.partial(project_kernel, chunks),
        out_shape=jax.ShapeDtypeStruct((2, width, TOK), F32),
        in_specs=[pl.BlockSpec(memory_space=pltpu.SMEM)] + [vmem] * 4,
        out_specs=anyspace,
        scratch_shapes=[
            pltpu.VMEM((2 * HALF, 2 * TOK), BF16),
            pltpu.VMEM((2, width, TOK), F32),
            pltpu.SemaphoreType.DMA((len(chunks), 2)),
        ],
        compiler_params=pltpu.CompilerParams(vmem_limit_bytes=LIMIT),
        cost_estimate=pl.CostEstimate(flops=3_000_000_000, bytes_accessed=14_000_000, transcendentals=0),
        name="project",
    )(timesteps, weight, gate_table, own, other)


def unpack_half(scale, packed, state_ref, total_ref):
    lanes = lax.broadcasted_iota(jnp.int32, (TROWS, LANES), 1)
    tiles = unpack_tiles(packed * scale)
    for head in range(HALF_HEADS):
        block = None
        for tile in tiles_of(head):
            low = max(HD * head, LANES * tile)
            turn = (HD * head - TILE_BASE[tile]) % LANES
            moved = pltpu.roll(tiles[tile], (LANES - turn) % LANES, 1) if turn else tiles[tile]
            block = moved if block is None else jnp.where(lanes >= low - HD * head, moved, block)
        total_ref[head : head + 1, :] = block[HD : HD + 1, :HD]
        state_ref[:, head, :] = block.T[:HD, :HD]


def own_kernel(scale, packed_ref, state_ref, total_ref):
    unpack_half(scale, packed_ref[...], state_ref, total_ref)


def rest_kernel(scale, packed_ref, own_state, own_total, state_out, total_out, state, total, sems):
    def stores(half, pair, n):
        spot = pl.ds(pl.multiple_of(half * HALF_HEADS, HALF_HEADS), HALF_HEADS)
        moves = [
            pltpu.make_async_copy(pair[0], state_out.at[:, spot], sems.at[n]),
            pltpu.make_async_copy(pair[1], total_out.at[spot], sems.at[n + 1]),
        ]
        for move in moves:
            move.start()
        return moves

    moves = stores(core_of(), (own_state, own_total), 0)
    unpack_half(scale, packed_ref[...], state, total)
    moves += stores(1 - core_of(), (state, total), 2)
    for move in moves:
        move.wait()


FRESH_COST = pl.CostEstimate(flops=1_000_000, bytes_accessed=600_000, transcendentals=0)


def fresh_own(packed, tokens):
    vmem = pl.BlockSpec(memory_space=pltpu.VMEM)
    return pl.pallas_call(
        functools.partial(own_kernel, 1.0 / tokens),
        out_shape=(jax.ShapeDtypeStruct((HD, HALF_HEADS, HD), F32), jax.ShapeDtypeStruct((HALF_HEADS, HD), F32)),
        in_specs=[vmem],
        out_specs=(vmem,) * 2,
        compiler_params=pltpu.CompilerParams(vmem_limit_bytes=4 << 20),
        cost_estimate=FRESH_COST,
        name="fresh_own",
    )(packed)


def fresh_rest(packed, own, tokens):
    vmem = pl.BlockSpec(memory_space=pltpu.VMEM)
    anyspace = pl.BlockSpec(memory_space=pl.ANY)
    return pl.pallas_call(
        functools.partial(rest_kernel, 1.0 / tokens),
        out_shape=(jax.ShapeDtypeStruct((HD, NH, HD), F32), jax.ShapeDtypeStruct((NH, HD), F32)),
        in_specs=[vmem] * 3,
        out_specs=(anyspace,) * 2,
        scratch_shapes=[
            pltpu.VMEM((HD, HALF_HEADS, HD), F32),
            pltpu.VMEM((HALF_HEADS, HD), F32),
            pltpu.SemaphoreType.DMA((4,)),
        ],
        compiler_params=pltpu.CompilerParams(vmem_limit_bytes=4 << 20),
        cost_estimate=FRESH_COST,
        name="fresh_rest",
    )(packed, *own)


def local(queries, keys, values, timesteps, gate_table, out_weight, conv_weight):
    count = lax.axis_size("tm")
    tokens = queries.shape[1] * count
    queries, keys, values = (x.transpose(0, 2, 1) for x in (queries, keys, values))
    far_keys, far_values = (pltpu.with_memory_space_constraint(x, pltpu.HBM) for x in (keys, values))

    def swap(x, pick):
        return lax.ppermute(x, "tm", [(i, i ^ pick(i % 2)) for i in range(count)])

    def partner(x):
        return swap(x, lambda c: 1)

    bits = [1 << b for b in range(1, count.bit_length() - 1)]

    parts = [bits[len(bits) * i // 3 : len(bits) * (i + 1) // 3] for i in range(3)]

    def rounds(even, odd):
        pairs = zip(*([b for i in order for b in parts[i]] for order in (even, odd)))
        return [lambda c, b=b, t=t: t if c else b for b, t in pairs]

    first = core_of() == 0
    (send0,) = local_states(far_keys, far_values, ((0, 0),))
    (keep0,) = held_states(keys, values, ((0, 1),))
    send1, keep1 = held_states(keys, values, ((1, 0), (1, 1)))
    plain, near, far, conv_weight = plain_values(values, conv_weight)
    near = partner(near)
    links = [p for i in range(1, count - 1, 2) for p in ((i, i + 1), (i + 1, i))]
    far = lax.ppermute(far, "tm", links)
    above, below = jnp.where(first, far, near), jnp.where(first, near, far)
    grid = plain.reshape(2, ROWS_DEV, COLS, plain.shape[-1])
    conv0 = convolve(jnp.concatenate([above[None], grid[0], below[None]], axis=0), conv_weight)
    again, above, below, weights, conv0 = lax.optimization_barrier((grid[1], above, below, conv_weight, conv0))
    conv1 = convolve(jnp.concatenate([above[None], again, below[None]], axis=0), weights)
    conv = turn(conv0, conv1)
    got0 = partner(send0)
    got1 = partner(send1)
    whole, second = keep0 + got0, keep1 + got1
    for pick in rounds(*FIRST_ORDERS):
        got = swap(whole, pick)
        whole = whole + got
    for pick in rounds(*SECOND_ORDERS):
        got = swap(second, pick)
        second = second + got
    other = partner(whole)
    staged = stage(pltpu.with_memory_space_constraint(out_weight, pltpu.HBM))
    own = spread(True, queries, conv, whole, keep0, keep1)
    rest = spread(False, queries, conv, other, send0, send1)
    update = project(timesteps, staged, gate_table, own, rest)
    other1 = partner(second)
    outs = fresh_own(second, tokens)
    fresh_state, fresh_total = fresh_rest(other1, outs, tokens)
    return update.transpose(0, 2, 1), fresh_state.transpose(1, 0, 2), fresh_total


def solution(mesh):
    placed = (
        P(None, ("grp", "tm"), None),
        P(None, ("grp", "tm"), None),
        P(None, ("grp", "tm"), None),
        P("grp"),
        P(),
        P(),
        P(),
    )

    return jax.shard_map(
        local,
        mesh=mesh,
        in_specs=placed,
        out_specs=(P(None, ("grp", "tm"), None), P("grp", None, None), P("grp", None)),
        check_vma=False,
    )
```

```python
import functools

import jax
import jax.numpy as jnp
from jax import lax
from jax.experimental import pallas as pl
from jax.experimental.pallas import tpu as pltpu
from jax.sharding import PartitionSpec as P


NH = 16
HD = 70
COLS = 64
ROWS_DEV = 4

F32 = jnp.float32
BF16 = jnp.bfloat16
LANES = 128
HALF_HEADS = NH // 2
HALF = HALF_HEADS * HD
TOK = ROWS_DEV * COLS
FULL_TILES = HALF // LANES
TILE_BASE = [LANES * j for j in range(FULL_TILES)] + [HALF - LANES]
REST = HALF - LANES * FULL_TILES
TROWS = 72
FOLD = 40
SLAB = 80
FIRST_ORDERS = (0, 1, 2), (1, 2, 0)
SECOND_ORDERS = (2, 0, 1), (0, 1, 2)
PACKED = FULL_TILES * TROWS + FOLD
LIMIT = 16 << 20


def core_of():
    return lax.rem(lax.axis_index("tm"), 2)


def tiles_of(head):
    first, last = HD * head, HD * head + HD
    return [j for j in range(FULL_TILES + 1) if first < min(LANES * j + LANES, HALF) and last > LANES * j]


def lane_mask(shape, tile, head):
    chan = TILE_BASE[tile] + lax.broadcasted_iota(jnp.int32, shape, 1)
    low = max(HD * head, LANES * tile)
    return (chan >= low) & (chan < HD * head + HD)


def nt_dot(a, b):
    return lax.dot_general(a, b, (((1,), (1,)), ((), ())), preferred_element_type=F32)


def pack_states(keys, values, out_ref):
    acc = [jnp.zeros((TROWS, LANES), F32) for _ in TILE_BASE]
    rows = lax.broadcasted_iota(jnp.int32, (TROWS, LANES), 0)
    ones = jnp.ones((16, TOK), BF16)
    for tile, base in enumerate(TILE_BASE):
        heads = [h for h in range(HALF_HEADS) if tile in tiles_of(h)]
        start = HD * heads[0] // 16 * 16
        stop = min(HALF, -(-(HD * heads[-1] + HD) // 16) * 16)
        prod = nt_dot(jnp.concatenate([values[start:stop], ones], axis=0), keys[base : base + LANES])
        for head in heads:
            shift = HD * head - start
            part = jnp.concatenate([prod[shift : shift + HD], jnp.zeros((TROWS - HD, LANES), F32)], axis=0)
            acc[tile] = jnp.where(lane_mask((TROWS, LANES), tile, head), part, acc[tile])
        total = prod[stop - start : stop - start + 1]
        acc[tile] = jnp.where(rows == HD, jnp.broadcast_to(total, (TROWS, LANES)), acc[tile])
    for tile in range(FULL_TILES):
        out_ref[tile * TROWS : (tile + 1) * TROWS] = acc[tile]
    last = acc[FULL_TILES]
    low = jnp.concatenate([last[FOLD:], jnp.zeros((2 * FOLD - TROWS, LANES), F32)], axis=0)
    lanes = lax.broadcasted_iota(jnp.int32, (FOLD, LANES), 1)
    out_ref[FULL_TILES * TROWS :] = jnp.where(lanes >= LANES - REST, last[:FOLD], pltpu.roll(low, LANES // 2, 1))


def unpack_tiles(packed):
    tiles = [packed[j * TROWS : (j + 1) * TROWS] for j in range(FULL_TILES)]
    fold = packed[FULL_TILES * TROWS :]
    tiles.append(jnp.concatenate([fold, pltpu.roll(fold, LANES // 2, 1)[: TROWS - FOLD]], axis=0))
    return tiles


def split2(x):
    one = x.astype(BF16)
    return one, (x - one.astype(F32)).astype(BF16)


def state_kernel(key_hbm, value_hbm, out_ref, key, value, sems):
    half = core_of()
    first = pl.ds(pl.multiple_of((1 - half) * HALF, HALF), HALF)
    later = pl.ds(pl.multiple_of(half * HALF, HALF), HALF)
    loads = []
    for n, spot in enumerate((first, later)):
        for m, (source, held) in enumerate(((key_hbm, key), (value_hbm, value))):
            loads.append(pltpu.make_async_copy(source.at[0, spot], held.at[spot], sems.at[n, m]))
            loads[-1].start()
    for load in loads[:2]:
        load.wait()
    pack_states(key[first], value[first], out_ref)
    for load in loads[2:]:
        load.wait()


def keep_kernel(key_hbm, value_hbm, key0, value0, out_ref, key, value, sems):
    loads = [
        pltpu.make_async_copy(key_hbm.at[1], key, sems.at[0]),
        pltpu.make_async_copy(value_hbm.at[1], value, sems.at[1]),
    ]
    for load in loads:
        load.start()
    own = pl.ds(pl.multiple_of(core_of() * HALF, HALF), HALF)
    pack_states(key0[own], value0[own], out_ref)
    for load in loads:
        load.wait()


def both_kernel(key, value, send_ref, keep_ref):
    for half, out_ref in ((1 - core_of(), send_ref), (core_of(), keep_ref)):
        spot = pl.ds(pl.multiple_of(half * HALF, HALF), HALF)
        pack_states(key[spot], value[spot], out_ref)


def local_states(kernel, sources, held, outs, sems):
    vmem = pl.BlockSpec(memory_space=pltpu.VMEM)
    packed = jax.ShapeDtypeStruct((PACKED, LANES), F32)
    copies = (jax.ShapeDtypeStruct(sources[0].shape[1:], BF16),) * 2 if sources else ()
    return pl.pallas_call(
        kernel,
        out_shape=(packed,) * outs + copies,
        in_specs=[pl.BlockSpec(memory_space=pltpu.HBM)] * len(sources) + [vmem] * len(held),
        out_specs=(vmem,) * (outs + len(copies)),
        scratch_shapes=[pltpu.SemaphoreType.DMA(sems)] if sems else [],
        compiler_params=pltpu.CompilerParams(vmem_limit_bytes=8 << 20),
        cost_estimate=pl.CostEstimate(flops=300_000_000 * outs, bytes_accessed=1_200_000, transcendentals=0),
    )(*sources, *held)


def plain_kernel(value0, value1, weight_ref, plain_ref, near_ref, far_ref, taps_ref):
    taps_ref[...] = weight_ref[...]
    first = core_of() == 0
    for step in range(2):
        plain_ref[step] = (value0, value1)[step][...].T
    head, tail = plain_ref[0, :COLS], plain_ref[0, TOK - COLS :]
    near_ref[...] = jnp.where(first, tail, head)
    far_ref[...] = jnp.where(first, head, tail)


def plain_values(values, weights):
    vmem = pl.BlockSpec(memory_space=pltpu.VMEM)
    width = values[0].shape[0]
    row = jax.ShapeDtypeStruct((COLS, width), BF16)
    return pl.pallas_call(
        plain_kernel,
        out_shape=(jax.ShapeDtypeStruct((2, TOK, width), BF16), row, row, jax.ShapeDtypeStruct(weights.shape, F32)),
        in_specs=[vmem] * 3,
        out_specs=(vmem,) * 4,
        compiler_params=pltpu.CompilerParams(vmem_limit_bytes=8 << 20),
        cost_estimate=pl.CostEstimate(flops=1_000_000, bytes_accessed=2_400_000, transcendentals=0),
        name="plain_values",
    )(*values, weights)


def convolve(padded, conv_weight):
    widened = jnp.pad(padded.astype(F32), ((0, 0), (1, 1), (0, 0)))
    summed = jnp.zeros((ROWS_DEV, COLS, padded.shape[-1]), F32)
    for tap_row in range(3):
        for tap_col in range(3):
            summed = (
                summed
                + widened[tap_row : tap_row + ROWS_DEV, tap_col : tap_col + COLS]
                * conv_weight[3 * tap_row + tap_col]
            )
    return summed.reshape(TOK, padded.shape[-1])


def spread_kernel(own, query, conv_ref, whole_ref, zero_ref, one_ref, out_ref, acc):
    half = core_of() if own else 1 - core_of()
    base = half * HALF
    whole = whole_ref[...]
    states = (whole, whole - zero_ref[...] + one_ref[...])
    rows8 = lax.broadcasted_iota(jnp.int32, (HALF_HEADS, LANES), 0)
    rows = lax.broadcasted_iota(jnp.int32, (TROWS, LANES), 0)
    for step in range(2):
        tiles = unpack_tiles(states[step])
        den = None
        sums = [None] * HALF_HEADS
        for tile, packed in enumerate(tiles):
            heads = [h for h in range(HALF_HEADS) if tile in tiles_of(h)]
            blocks = []
            for head in heads:
                shift = HD * head % 8
                block = jnp.where(lane_mask((TROWS, LANES), tile, head) & (rows < HD), packed, 0.0)
                block = jnp.concatenate([block, jnp.zeros((SLAB - TROWS, LANES), F32)], axis=0)
                if shift:
                    block = jnp.concatenate([block[SLAB - shift :], block[: SLAB - shift]], axis=0)
                blocks.append(block)
            owner = jnp.zeros((HALF_HEADS, LANES), jnp.int32)
            for head in heads:
                owner = jnp.where(lane_mask((HALF_HEADS, LANES), tile, head) & (rows8 == head), 1, owner)
            row = jnp.where(owner == 1, jnp.broadcast_to(packed[HD : HD + 1], (HALF_HEADS, LANES)), 0.0)
            blocks += [row, jnp.zeros((HALF_HEADS, LANES), F32)]
            left = jnp.concatenate(split2(jnp.concatenate(blocks, axis=0)), axis=1)
            q = query[step, pl.ds(pl.multiple_of(base + TILE_BASE[tile], 16), LANES)]
            got = jnp.dot(left, jnp.concatenate([q, q], axis=0), preferred_element_type=F32)
            for n, head in enumerate(heads):
                part_sum = got[n * SLAB : (n + 1) * SLAB]
                sums[head] = part_sum if sums[head] is None else sums[head] + part_sum
            part_den = got[len(heads) * SLAB : len(heads) * SLAB + HALF_HEADS]
            den = part_den if den is None else den + part_den
        inverse = 1.0 / den
        acc[...] = jnp.zeros((HALF, TOK), F32)
        for head in range(HALF_HEADS):
            first = HD * head // 8 * 8
            count = -(-(HD * head - first + HD) // 8) * 8
            spot = slice(first, first + count)
            acc[spot] = acc[spot] + sums[head][:count] * inverse[head : head + 1]
        conv = conv_ref[step, pl.ds(pl.multiple_of(base, HALF), HALF)]
        out_ref[:, step * TOK : (step + 1) * TOK] = (acc[...] + conv).astype(BF16)


def spread(own, queries, conv, whole, zero, one):
    vmem = pl.BlockSpec(memory_space=pltpu.VMEM)
    return pl.pallas_call(
        functools.partial(spread_kernel, own),
        out_shape=jax.ShapeDtypeStruct((HALF, 2 * TOK), BF16),
        in_specs=[vmem] * 5,
        out_specs=vmem,
        scratch_shapes=[pltpu.VMEM((HALF, TOK), F32)],
        compiler_params=pltpu.CompilerParams(vmem_limit_bytes=8 << 20),
        cost_estimate=pl.CostEstimate(flops=800_000_000, bytes_accessed=2_000_000, transcendentals=0),
        name="spread",
    )(queries, conv, whole, zero, one)


def turn_kernel(conv0, conv1, out_ref):
    for step, conv in enumerate((conv0, conv1)):
        out_ref[step] = conv[...].T


def turn(conv0, conv1):
    tokens, width = conv0.shape
    vmem = pl.BlockSpec(memory_space=pltpu.VMEM)
    return pl.pallas_call(
        turn_kernel,
        out_shape=jax.ShapeDtypeStruct((2, width, tokens), F32),
        in_specs=[vmem] * 2,
        out_specs=vmem,
        compiler_params=pltpu.CompilerParams(vmem_limit_bytes=8 << 20),
        cost_estimate=pl.CostEstimate(flops=1_000_000, bytes_accessed=4_600_000, transcendentals=0),
        name="turn",
    )(conv0, conv1)


def project_kernel(chunks, step_ref, weight, gate_ref, own_ref, other_ref, out_hbm, mixed, result, sem_out):
    half = core_of()
    for at, part in ((half, own_ref), (1 - half, other_ref)):
        mixed[pl.ds(pl.multiple_of(at * HALF, HALF), HALF)] = part[...]
    gate_rows = [gate_ref[pl.ds(step_ref[s], 1), :] for s in range(2)]
    gates = jnp.concatenate(gate_rows + [gate_rows[0]] * 6, axis=0).T
    stores = []
    for n, (start, size) in enumerate(chunks):
        prod = lax.dot_general(
            weight[:, start : start + size], mixed[...], (((0,), (0,)), ((), ())), preferred_element_type=F32
        )
        for step in range(2):
            result[step, start : start + size] = (
                prod[:, step * TOK : (step + 1) * TOK] * gates[start : start + size, step : step + 1]
            )
            stores.append(
                pltpu.make_async_copy(
                    result.at[step, start : start + size], out_hbm.at[step, start : start + size], sem_out.at[n, step]
                )
            )
            stores[-1].start()
    for store in stores:
        store.wait()


def stage_kernel(weight_hbm, out_ref, sem):
    load = pltpu.make_async_copy(weight_hbm, out_ref, sem)
    load.start()
    load.wait()


def stage(weight):
    return pl.pallas_call(
        stage_kernel,
        out_shape=jax.ShapeDtypeStruct(weight.shape, weight.dtype),
        in_specs=[pl.BlockSpec(memory_space=pltpu.HBM)],
        out_specs=pl.BlockSpec(memory_space=pltpu.VMEM),
        scratch_shapes=[pltpu.SemaphoreType.DMA],
        compiler_params=pltpu.CompilerParams(vmem_limit_bytes=8 << 20),
        cost_estimate=pl.CostEstimate(flops=0, bytes_accessed=5_000_000, transcendentals=0),
        name="stage",
    )(weight)


def project(timesteps, weight, gate_table, own, other):
    width = weight.shape[1]
    chunks = [(s, min(256, width - s)) for s in range(0, width, 256)]
    vmem = pl.BlockSpec(memory_space=pltpu.VMEM)
    anyspace = pl.BlockSpec(memory_space=pl.ANY)
    return pl.pallas_call(
        functools.partial(project_kernel, chunks),
        out_shape=jax.ShapeDtypeStruct((2, width, TOK), F32),
        in_specs=[pl.BlockSpec(memory_space=pltpu.SMEM)] + [vmem] * 4,
        out_specs=anyspace,
        scratch_shapes=[
            pltpu.VMEM((2 * HALF, 2 * TOK), BF16),
            pltpu.VMEM((2, width, TOK), F32),
            pltpu.SemaphoreType.DMA((len(chunks), 2)),
        ],
        compiler_params=pltpu.CompilerParams(vmem_limit_bytes=LIMIT),
        cost_estimate=pl.CostEstimate(flops=3_000_000_000, bytes_accessed=14_000_000, transcendentals=0),
        name="project",
    )(timesteps, weight, gate_table, own, other)


def unpack_half(scale, packed, state_ref, total_ref):
    lanes = lax.broadcasted_iota(jnp.int32, (TROWS, LANES), 1)
    tiles = unpack_tiles(packed * scale)
    for head in range(HALF_HEADS):
        block = None
        for tile in tiles_of(head):
            low = max(HD * head, LANES * tile)
            turn = (HD * head - TILE_BASE[tile]) % LANES
            moved = pltpu.roll(tiles[tile], (LANES - turn) % LANES, 1) if turn else tiles[tile]
            block = moved if block is None else jnp.where(lanes >= low - HD * head, moved, block)
        total_ref[head : head + 1, :] = block[HD : HD + 1, :HD]
        state_ref[:, head, :] = block.T[:HD, :HD]


def own_kernel(scale, packed_ref, state_ref, total_ref):
    unpack_half(scale, packed_ref[...], state_ref, total_ref)


def rest_kernel(scale, packed_ref, own_state, own_total, state_out, total_out, state, total, sems):
    def stores(half, pair, n):
        spot = pl.ds(pl.multiple_of(half * HALF_HEADS, HALF_HEADS), HALF_HEADS)
        moves = [
            pltpu.make_async_copy(pair[0], state_out.at[:, spot], sems.at[n]),
            pltpu.make_async_copy(pair[1], total_out.at[spot], sems.at[n + 1]),
        ]
        for move in moves:
            move.start()
        return moves

    moves = stores(core_of(), (own_state, own_total), 0)
    unpack_half(scale, packed_ref[...], state, total)
    moves += stores(1 - core_of(), (state, total), 2)
    for move in moves:
        move.wait()


FRESH_COST = pl.CostEstimate(flops=1_000_000, bytes_accessed=600_000, transcendentals=0)


def fresh_own(packed, tokens):
    vmem = pl.BlockSpec(memory_space=pltpu.VMEM)
    return pl.pallas_call(
        functools.partial(own_kernel, 1.0 / tokens),
        out_shape=(jax.ShapeDtypeStruct((HD, HALF_HEADS, HD), F32), jax.ShapeDtypeStruct((HALF_HEADS, HD), F32)),
        in_specs=[vmem],
        out_specs=(vmem,) * 2,
        compiler_params=pltpu.CompilerParams(vmem_limit_bytes=4 << 20),
        cost_estimate=FRESH_COST,
        name="fresh_own",
    )(packed)


def fresh_rest(packed, own, tokens):
    vmem = pl.BlockSpec(memory_space=pltpu.VMEM)
    anyspace = pl.BlockSpec(memory_space=pl.ANY)
    return pl.pallas_call(
        functools.partial(rest_kernel, 1.0 / tokens),
        out_shape=(jax.ShapeDtypeStruct((HD, NH, HD), F32), jax.ShapeDtypeStruct((NH, HD), F32)),
        in_specs=[vmem] * 3,
        out_specs=(anyspace,) * 2,
        scratch_shapes=[
            pltpu.VMEM((HD, HALF_HEADS, HD), F32),
            pltpu.VMEM((HALF_HEADS, HD), F32),
            pltpu.SemaphoreType.DMA((4,)),
        ],
        compiler_params=pltpu.CompilerParams(vmem_limit_bytes=4 << 20),
        cost_estimate=FRESH_COST,
        name="fresh_rest",
    )(packed, *own)


def local(queries, keys, values, timesteps, gate_table, out_weight, conv_weight):
    count = lax.axis_size("tm")
    tokens = queries.shape[1] * count
    queries, keys, values = (x.transpose(0, 2, 1) for x in (queries, keys, values))
    far_keys, far_values = (pltpu.with_memory_space_constraint(x, pltpu.HBM) for x in (keys, values))

    def swap(x, pick):
        return lax.ppermute(x, "tm", [(i, i ^ pick(i % 2)) for i in range(count)])

    def partner(x):
        return swap(x, lambda c: 1)

    bits = [1 << b for b in range(1, count.bit_length() - 1)]

    parts = [bits[len(bits) * i // 3 : len(bits) * (i + 1) // 3] for i in range(3)]

    def rounds(even, odd):
        pairs = zip(*([b for i in order for b in parts[i]] for order in (even, odd)))
        return [lambda c, b=b, t=t: t if c else b for b, t in pairs]

    first = core_of() == 0
    sources = far_keys, far_values
    send0, *held0 = local_states(state_kernel, sources, (), 1, (2, 2))
    keep0, *held1 = local_states(keep_kernel, sources, held0, 1, (2,))
    send1, keep1 = local_states(both_kernel, (), held1, 2, None)
    plain, near, far, conv_weight = plain_values((held0[1], held1[1]), conv_weight)
    near = partner(near)
    links = [p for i in range(1, count - 1, 2) for p in ((i, i + 1), (i + 1, i))]
    far = lax.ppermute(far, "tm", links)
    above, below = jnp.where(first, far, near), jnp.where(first, near, far)
    grid = plain.reshape(2, ROWS_DEV, COLS, plain.shape[-1])
    conv0 = convolve(jnp.concatenate([above[None], grid[0], below[None]], axis=0), conv_weight)
    again, above, below, weights, conv0 = lax.optimization_barrier((grid[1], above, below, conv_weight, conv0))
    conv1 = convolve(jnp.concatenate([above[None], again, below[None]], axis=0), weights)
    conv = turn(conv0, conv1)
    got0 = partner(send0)
    got1 = partner(send1)
    whole, second = keep0 + got0, keep1 + got1
    for pick in rounds(*FIRST_ORDERS):
        got = swap(whole, pick)
        whole = whole + got
    for pick in rounds(*SECOND_ORDERS):
        got = swap(second, pick)
        second = second + got
    other = partner(whole)
    staged = stage(pltpu.with_memory_space_constraint(out_weight, pltpu.HBM))
    own = spread(True, queries, conv, whole, keep0, keep1)
    rest = spread(False, queries, conv, other, send0, send1)
    update = project(timesteps, staged, gate_table, own, rest)
    other1 = partner(second)
    outs = fresh_own(second, tokens)
    fresh_state, fresh_total = fresh_rest(other1, outs, tokens)
    return update.transpose(0, 2, 1), fresh_state.transpose(1, 0, 2), fresh_total


def solution(mesh):
    placed = (
        P(None, ("grp", "tm"), None),
        P(None, ("grp", "tm"), None),
        P(None, ("grp", "tm"), None),
        P("grp"),
        P(),
        P(),
        P(),
    )

    return jax.shard_map(
        local,
        mesh=mesh,
        in_specs=placed,
        out_specs=(P(None, ("grp", "tm"), None), P("grp", None, None), P("grp", None)),
        check_vma=False,
    )
```
